32 devices in a mesh: groups: 2 (over y), dp: 2 (over x), expert: 8 (over z, core).
Axes of the slice: x: 2, y: 2, z: 4, core: 2. Of those that a mesh axis runs over, the one named last changes fastest.
Arguments:
- tokens: bfloat16 [4096, 2048], P(('groups', 'dp', 'expert')), parts along dimension 0, may hold values from -6 to 6
- routes: int32 [4096, 4], P(('groups', 'dp', 'expert')), parts along dimension 0, may hold values from 0 to 7, all different within a row; in each aligned block of 128 rows (0 to 127, 128 to 255, ...) at most 128 rows name the same one
- w_gate: bfloat16 [16, 2048, 512], P(('groups', 'expert')), parts along dimension 0, may hold values from -0.125 to 0.125
- w_up: bfloat16 [16, 2048, 512], P(('groups', 'expert')), parts along dimension 0, may hold values from -0.125 to 0.125
Outputs:
- r_factor: float32 [16, 512, 512], P(('groups', 'expert'), 'dp'), parts along dimension 0
The draws below stay inside these ranges and needn't reach their ends.
There are 2 independent parts, one for each index of `groups`. The reference program is written for one: setup_inputs(seed, part) draws one part's arguments, and reference() takes and returns one part's arrays. A program takes and returns all parts, laid end to end along the dimension named above; each array names one. Nothing has to cross between parts.
Inputs may be any that keep to these rules, and one draw needn't show every extreme that they name: `routes`: each row names 4 different experts. In each aligned block of 128 rows (the tokens of one device) no expert is named by more than 128 rows, and in some block some expert is named by exactly 128 rows.
All inputs are finite; a program needn't handle non-finite values.
Results may differ from the reference program's by a relative error of at most 0.0027.
Values may be sent and summed in bfloat16 or wider, within the bound.
No kernel may reach another device: no remote copies, remote signals or barrier semaphores. Data moves between devices by JAX's collectives and lax.ppermute only.
A program may use at most 64 MiB of HBM per device.

```python
import math
import jax
import jax.numpy as jnp
import numpy as np
from jax import lax

D = 2048
HW = 512
T_DEV = 128
TOPK = 4
EXPERTS = 8
CAP = 128
ROWS_MEAN = 1024
TOKENS = 2048
N_DP = 2
N_EXPERT = 8


def shard_levels(stream_key, dims, cuts, least, top_value):
    loudness, own = 1.0, jax.random.fold_in(stream_key, 6)
    for axis_at, blocks in cuts:
        steps = jnp.exp(jax.random.uniform(jax.random.fold_in(own, axis_at), (blocks,), jnp.float32, least / len(cuts), top_value / len(cuts)))
        loudness = loudness * jnp.repeat(steps, dims[axis_at] // blocks).reshape([-1 if axis == axis_at else 1 for axis in range(len(dims))])
    return loudness


def assign_block(stream_key, own, number, rows, count, top, bound, skew):
    ranking = jax.random.permutation(stream_key, count)
    packed, usual = portions_of(count, rows * top, bound, skew, True), portions_of(count, rows * top, bound, skew, False)
    places = jnp.arange(count)

    def named(sizes, offset_by):
        used = int((sizes > 0).sum())
        fixed = max(1, used // 4)
        moved = fixed + (places - fixed + offset_by * (used - fixed)) % max(1, count - fixed)
        return jnp.zeros((count,), jnp.int32).at[ranking[jnp.where(places < fixed, places, moved)]].set(jnp.asarray(sizes, jnp.int32))

    sizes = jnp.where(number % 4 == 0, named(packed, number // 4), named(usual, number - number // 4 - 1))
    mixed = jax.random.permutation(jax.random.fold_in(own, 3), count)
    giver, receiver = mixed[0:count // 2 * 2:2], mixed[1:count // 2 * 2:2]
    room = jnp.minimum(sizes[giver] - 1, bound - sizes[receiver]) // 2
    room = jnp.where((giver == ranking[0]) | (receiver == ranking[0]) | (sizes[receiver] == 0), 0, jnp.maximum(room, 0))
    moved = jax.random.randint(jax.random.fold_in(own, 4), (count // 2,), 0, 1 << 20) % (room + 1)
    sizes = sizes.at[giver].add(-moved).at[receiver].add(moved)
    labels = jnp.searchsorted(jnp.cumsum(sizes), jnp.arange(rows * top), side="right").astype(jnp.int32)
    grid = labels.reshape(top, rows).T
    grid = grid[jax.random.permutation(jax.random.fold_in(own, 1), rows)]
    offset_by = jax.random.randint(jax.random.fold_in(own, 2), (rows, 1), 0, top)
    return jnp.take_along_axis(grid, (jnp.arange(top)[None, :] + offset_by) % top, axis=1)


def portions_of(amount, total, limit, slope, full):
    loads = [(1 << 20) // math.isqrt(grade ** slope) + 1 for grade in range(1, amount + 1)]
    largest = limit if full else min(limit, max(-(-total // amount), total * loads[0] // sum(loads)))
    least = 1 if total - largest >= amount - 1 else 0
    holding, spare = [largest] + [least] * (amount - 1), total - largest - least * (amount - 1)
    while spare > 0:
        candidates = [i for i in range(1, amount) if holding[i] < largest] or [i for i in range(1, amount) if holding[i] < limit]
        pool, budget = sum([loads[i] for i in candidates]), spare
        for i in candidates:
            addition = min(limit - holding[i], max(1, budget * loads[i] // pool), spare)
            holding[i] = holding[i] + addition
            spare = spare - addition
    return np.array(holding)


def scatter_about(own_key, shape, deviation, bound, pieces=(), kind=jnp.bfloat16):
    entries = jax.random.normal(own_key, shape, jnp.float32) * deviation
    if len(pieces) > 0:
        entries = shard_levels(own_key, shape, pieces, -0.22, 0.18) * entries
    return jnp.clip(entries, min=-bound, max=bound).astype(kind)


def setup_inputs(seed: int = 0, part: int = 0) -> dict:
    streams_of = jax.random.split(jax.random.key(seed), 5)
    part_splits = jax.random.split(jax.random.fold_in(streams_of[4], part), 5)
    tokens = scatter_about(part_splits[0], (TOKENS, D), 1.0, 6.0, ((0, 16),))
    routes_keys = jax.random.split(jax.random.fold_in(part_splits[1], 1), TOKENS // T_DEV)
    routes_turns = jax.random.permutation(jax.random.fold_in(part_splits[1], 3), TOKENS // T_DEV)
    routes = jax.vmap(lambda own, number: assign_block(jax.random.fold_in(part_splits[1], 2), own, number, T_DEV, EXPERTS, TOPK, CAP, 2))(routes_keys, routes_turns).reshape((TOKENS, TOPK))
    w_gate = scatter_about(part_splits[2], (EXPERTS, D, HW), D ** -0.5, 0.125, ((0, 8),))
    w_up = scatter_about(part_splits[3], (EXPERTS, D, HW), D ** -0.5, 0.125, ((0, 8),))
    return dict(tokens=tokens, routes=routes, w_gate=w_gate, w_up=w_up)


RIDGE = 0.05

def reference(tokens, routes, w_gate, w_up):
    row_limit = N_DP * N_EXPERT * CAP

    def per_expert(expert_id):
        member = jnp.any(routes == expert_id, axis=1)
        row_ids = jnp.nonzero(member, size=row_limit, fill_value=0)[0].astype(jnp.int32)
        valid = jnp.arange(row_limit, dtype=jnp.int32) < jnp.sum(member.astype(jnp.int32))
        picked = tokens[row_ids]
        gate_proj = jnp.dot(picked.astype(jnp.float32), w_gate[expert_id].astype(jnp.float32), preferred_element_type=jnp.float32)
        up_proj = jnp.dot(picked.astype(jnp.float32), w_up[expert_id].astype(jnp.float32), preferred_element_type=jnp.float32)
        hidden = jnp.where(valid[:, None], jax.nn.silu(gate_proj) * up_proj, 0.0).astype(jnp.bfloat16)
        gram_local = lax.dot_general(hidden.astype(jnp.float32), hidden.astype(jnp.float32), (((0,), (0,)), ((), ())), preferred_element_type=jnp.float32)
        regular = gram_local / ROWS_MEAN + RIDGE * jnp.eye(HW, dtype=jnp.float32)
        return jnp.linalg.cholesky(regular).T
    return lax.map(per_expert, jnp.arange(EXPERTS, dtype=jnp.int32))
```

```python
import functools

import jax
import jax.numpy as jnp
from jax import lax
from jax.experimental import pallas as pl
from jax.experimental.pallas import tpu as pltpu
from jax.sharding import PartitionSpec as P

RIDGE = 0.05
CORES = 2


def hidden_gram_kernel(own_ref, other_ref, member_ref, gate_ref, up_ref, *rest):
    first = len(rest) == 2
    gram_in_ref = None if first else rest[0]
    gram_ref, hidden_ref = rest[-2:]
    step = pl.program_id(0)
    rows = own_ref.shape[0]
    width = gate_ref.shape[1]
    gate_block = gate_ref[...]
    up_block = up_ref[...]
    x = jnp.concatenate([own_ref[...], other_ref[...]], axis=0)
    gate = jnp.dot(x, gate_block, preferred_element_type=jnp.float32)
    up = jnp.dot(x, up_block, preferred_element_type=jnp.float32)
    value = gate / (1.0 + jnp.exp(-gate)) * up
    value = jnp.where(member_ref[...] > 0, value, 0.0)
    hidden_ref[:, pl.ds(pl.multiple_of(step * width, width), width)] = value.astype(jnp.bfloat16)

    @pl.when(step == pl.num_programs(0) - 1)
    def _():
        h = hidden_ref[...]
        gram = lax.dot_general(h, h, (((0,), (0,)), ((), ())), preferred_element_type=jnp.float32)
        if first:
            gram_ref[...] = gram
        else:
            gram_ref[...] = gram_in_ref[...] + gram


def hidden_gram(own, other, member, slot, gate_w, up_w, gram=None, width=256):
    rows, model = own.shape
    hw = gate_w.shape[1]
    whole = lambda i: (0, 0)
    in_specs = [
        pl.BlockSpec((rows, model), whole),
        pl.BlockSpec((rows, model), whole),
        pl.BlockSpec((2 * rows, 1), lambda i: (slot, 0)),
        pl.BlockSpec((model, width), lambda i: (0, i)),
        pl.BlockSpec((model, width), lambda i: (0, i)),
    ]
    args = [own, other, member, gate_w, up_w]
    aliases = {}
    if gram is not None:
        in_specs.append(pl.BlockSpec((hw, hw), whole))
        args.append(gram)
        aliases = {5: 0}
    return pl.pallas_call(
        hidden_gram_kernel,
        grid=(hw // width,),
        in_specs=in_specs,
        out_specs=pl.BlockSpec((hw, hw), whole),
        out_shape=jax.ShapeDtypeStruct((hw, hw), jnp.float32),
        scratch_shapes=[pltpu.VMEM((2 * rows, hw), jnp.bfloat16)],
        input_output_aliases=aliases,
        compiler_params=pltpu.CompilerParams(dimension_semantics=("arbitrary",)),
        cost_estimate=pl.CostEstimate(
            flops=2 * 2 * rows * model * 2 * hw + 2 * 2 * rows * hw * hw,
            bytes_accessed=2 * (2 * rows * model + 2 * model * hw) + 4 * hw * hw,
            transcendentals=2 * rows * hw,
        ),
        name=f"hidden_gram_{slot}",
    )(*args)


def shifted(pairs):
    return [(s * CORES + c, d * CORES + c) for s, d in pairs for c in range(CORES)]


def gather_grams(tokens, routes, gate_w, up_w):
    owners = lax.axis_size("expert")
    chips = owners // CORES
    me = lax.axis_index("expert")
    move = lambda x, pairs: lax.ppermute(x, "expert", pairs)
    swap = [(e, e ^ 1) for e in range(owners)]
    ring = lambda s: shifted([(z, (z + s) % chips) for z in range(chips)])

    direct = {}
    if chips == 4:
        direct[1] = move(tokens, ring(1))
        direct[3] = move(tokens, ring(-1))
        far = move(tokens, shifted([(0, 2), (3, 1)]))
        on_up = move(direct[1], shifted([(2, 3)]))
        on_down = move(direct[3], shifted([(1, 0)]))
        direct[2] = far + on_up + on_down
    else:
        for s in range(1, chips):
            direct[s] = move(tokens, ring(s))

    names = routes.T
    pair = jnp.concatenate([names, move(names, swap)], axis=0)
    named = [pair] + [move(pair, ring(s)) for s in range(1, chips)]
    named = jnp.stack(named).reshape(chips, CORES, routes.shape[1], routes.shape[0])
    member = jnp.any(named == me, axis=2).astype(jnp.float32).reshape(-1, 1)

    gram = hidden_gram(tokens, move(tokens, swap), member, 0, gate_w, up_w)
    order = [1, 3, 2] if chips == 4 else list(range(1, chips))
    for s in order:
        gram = hidden_gram(direct[s], move(direct[s], swap), member, s, gate_w, up_w, gram)
    return gram


def packed_grams(tokens, routes, gate_w, up_w, capacity):
    owners = lax.axis_size("expert")
    experts = owners
    model_width = tokens.shape[1]
    tok_rows, top_count = routes.shape
    assigned = routes.reshape(-1)
    onehot = (assigned[:, None] == jnp.arange(experts, dtype=jnp.int32)[None, :]).astype(jnp.int32)
    position = jnp.sum(jnp.cumsum(onehot, axis=0) * onehot, axis=1) - 1
    target = assigned * capacity + position
    anchor = jnp.arange(tok_rows * top_count, dtype=jnp.int32) // top_count
    source_row = jnp.zeros((experts * capacity,), jnp.int32).at[target].set(anchor)
    filled = jnp.zeros((experts * capacity,), jnp.int32).at[target].set(1)
    outbox = jnp.where(filled[:, None] > 0, tokens[source_row], jnp.zeros((), tokens.dtype))
    outbox = outbox.reshape(experts, capacity, model_width)
    arrived = lax.all_to_all(outbox, "expert", split_axis=0, concat_axis=0, tiled=True)
    flattened = arrived.reshape(-1, model_width)
    gate_proj = jnp.dot(flattened, gate_w, preferred_element_type=jnp.float32)
    up_proj = jnp.dot(flattened, up_w, preferred_element_type=jnp.float32)
    hidden = (jax.nn.silu(gate_proj) * up_proj).astype(jnp.bfloat16)
    return lax.dot_general(hidden, hidden, (((0,), (0,)), ((), ())), preferred_element_type=jnp.float32)


def body(tokens, routes, w_gate, w_up):
    owners = lax.axis_size("expert")
    data_ranks = lax.axis_size("dp")
    experts = w_gate.shape[0] * owners
    factor_width = w_gate.shape[2]
    tok_rows, top_count = routes.shape
    capacity = min(tok_rows, 2 * tok_rows * top_count // experts)
    gate_w, up_w = w_gate[0], w_up[0]
    if tok_rows * owners <= experts * capacity and owners % CORES == 0:
        gram_local = gather_grams(tokens, routes, gate_w, up_w)
    else:
        gram_local = packed_grams(tokens, routes, gate_w, up_w, capacity)
    rows_mean = data_ranks * tok_rows * top_count
    return finish(gram_local, rows_mean, data_ranks, factor_width)


def finish(gram_local, rows_mean, data_ranks, factor_width):
    block_rows = factor_width // data_ranks
    my_rank = lax.axis_index("dp")
    summed = gram_local
    for s in range(1, data_ranks):
        summed = summed + lax.ppermute(gram_local, "dp", [(r, (r + s) % data_ranks) for r in range(data_ranks)])
    regular = summed / rows_mean + RIDGE * jnp.eye(factor_width, dtype=jnp.float32)
    factor = jnp.linalg.cholesky(regular).T
    my_rows = lax.dynamic_slice_in_dim(factor, my_rank * block_rows, block_rows, 0)
    return my_rows.reshape(1, block_rows, factor_width)


def solution(mesh):
    in_specs = (
        P(("groups", "dp", "expert"), None),
        P(("groups", "dp", "expert"), None),
        P(("groups", "expert"), None, None),
        P(("groups", "expert"), None, None),
    )
    out_specs = P(("groups", "expert"), "dp", None)
    return jax.shard_map(body, mesh=mesh, in_specs=in_specs, out_specs=out_specs, check_vma=False)
```

```python
import functools

import jax
import jax.numpy as jnp
from jax import lax
from jax.experimental import pallas as pl
from jax.experimental.pallas import tpu as pltpu
from jax.sharding import PartitionSpec as P

RIDGE = 0.05
CORES = 2


def hidden_gram_kernel(own_ref, other_ref, member_ref, gate_ref, up_ref, *rest):
    first = len(rest) == 2
    gram_in_ref = None if first else rest[0]
    gram_ref, hidden_ref = rest[-2:]
    step = pl.program_id(0)
    rows = own_ref.shape[0]
    width = gate_ref.shape[1]
    gate_block = gate_ref[...]
    up_block = up_ref[...]
    x = jnp.concatenate([own_ref[...], other_ref[...]], axis=0)
    gate = jnp.dot(x, gate_block, preferred_element_type=jnp.float32)
    up = jnp.dot(x, up_block, preferred_element_type=jnp.float32)
    value = gate / (1.0 + jnp.exp(-gate)) * up
    value = jnp.where(member_ref[...] > 0, value, 0.0)
    hidden_ref[:, pl.ds(pl.multiple_of(step * width, width), width)] = value.astype(jnp.bfloat16)

    @pl.when(step == pl.num_programs(0) - 1)
    def _():
        h = hidden_ref[...]
        gram = lax.dot_general(h, h, (((0,), (0,)), ((), ())), preferred_element_type=jnp.float32)
        if first:
            gram_ref[...] = gram
        else:
            gram_ref[...] = gram_in_ref[...] + gram


def hidden_gram(own, other, member, slot, gate_w, up_w, gram=None, width=256):
    rows, model = own.shape
    hw = gate_w.shape[1]
    whole = lambda i: (0, 0)
    in_specs = [
        pl.BlockSpec((rows, model), whole),
        pl.BlockSpec((rows, model), whole),
        pl.BlockSpec((2 * rows, 1), lambda i: (slot, 0)),
        pl.BlockSpec((model, width), lambda i: (0, i)),
        pl.BlockSpec((model, width), lambda i: (0, i)),
    ]
    args = [own, other, member, gate_w, up_w]
    aliases = {}
    if gram is not None:
        in_specs.append(pl.BlockSpec((hw, hw), whole))
        args.append(gram)
        aliases = {5: 0}
    return pl.pallas_call(
        hidden_gram_kernel,
        grid=(hw // width,),
        in_specs=in_specs,
        out_specs=pl.BlockSpec((hw, hw), whole),
        out_shape=jax.ShapeDtypeStruct((hw, hw), jnp.float32),
        scratch_shapes=[pltpu.VMEM((2 * rows, hw), jnp.bfloat16)],
        input_output_aliases=aliases,
        compiler_params=pltpu.CompilerParams(dimension_semantics=("arbitrary",)),
        cost_estimate=pl.CostEstimate(
            flops=2 * 2 * rows * model * 2 * hw + 2 * 2 * rows * hw * hw,
            bytes_accessed=2 * (2 * rows * model + 2 * model * hw) + 4 * hw * hw,
            transcendentals=2 * rows * hw,
        ),
        name=f"hidden_gram_{slot}",
    )(*args)


def shifted(pairs):
    return [(s * CORES + c, d * CORES + c) for s, d in pairs for c in range(CORES)]


def gather_grams(tokens, routes, gate_w, up_w):
    owners = lax.axis_size("expert")
    chips = owners // CORES
    me = lax.axis_index("expert")
    move = lambda x, pairs: lax.ppermute(x, "expert", pairs)
    swap = [(e, e ^ 1) for e in range(owners)]
    ring = lambda s: shifted([(z, (z + s) % chips) for z in range(chips)])

    direct = {}
    if chips == 4:
        direct[1] = move(tokens, ring(1))
        direct[3] = move(tokens, ring(-1))
        far = move(tokens, shifted([(0, 2), (3, 1)]))
        on_up = move(direct[1], shifted([(2, 3)]))
        on_down = move(direct[3], shifted([(1, 0)]))
        direct[2] = far + on_up + on_down
    else:
        for s in range(1, chips):
            direct[s] = move(tokens, ring(s))

    names = routes.T
    pair = jnp.concatenate([names, move(names, swap)], axis=0)
    named = [pair] + [move(pair, ring(s)) for s in range(1, chips)]
    named = jnp.stack(named).reshape(chips, CORES, routes.shape[1], routes.shape[0])
    member = jnp.any(named == me, axis=2).astype(jnp.float32).reshape(-1, 1)

    gram = hidden_gram(tokens, move(tokens, swap), member, 0, gate_w, up_w)
    order = [1, 3, 2] if chips == 4 else list(range(1, chips))
    for s in order:
        gram = hidden_gram(direct[s], move(direct[s], swap), member, s, gate_w, up_w, gram)
    return gram


def packed_grams(tokens, routes, gate_w, up_w, capacity):
    owners = lax.axis_size("expert")
    experts = owners
    model_width = tokens.shape[1]
    tok_rows, top_count = routes.shape
    assigned = routes.reshape(-1)
    onehot = (assigned[:, None] == jnp.arange(experts, dtype=jnp.int32)[None, :]).astype(jnp.int32)
    position = jnp.sum(jnp.cumsum(onehot, axis=0) * onehot, axis=1) - 1
    target = assigned * capacity + position
    anchor = jnp.arange(tok_rows * top_count, dtype=jnp.int32) // top_count
    source_row = jnp.zeros((experts * capacity,), jnp.int32).at[target].set(anchor)
    filled = jnp.zeros((experts * capacity,), jnp.int32).at[target].set(1)
    outbox = jnp.where(filled[:, None] > 0, tokens[source_row], jnp.zeros((), tokens.dtype))
    outbox = outbox.reshape(experts, capacity, model_width)
    arrived = lax.all_to_all(outbox, "expert", split_axis=0, concat_axis=0, tiled=True)
    flattened = arrived.reshape(-1, model_width)
    gate_proj = jnp.dot(flattened, gate_w, preferred_element_type=jnp.float32)
    up_proj = jnp.dot(flattened, up_w, preferred_element_type=jnp.float32)
    hidden = (jax.nn.silu(gate_proj) * up_proj).astype(jnp.bfloat16)
    return lax.dot_general(hidden, hidden, (((0,), (0,)), ((), ())), preferred_element_type=jnp.float32)


def body(tokens, routes, w_gate, w_up):
    owners = lax.axis_size("expert")
    data_ranks = lax.axis_size("dp")
    experts = w_gate.shape[0] * owners
    factor_width = w_gate.shape[2]
    tok_rows, top_count = routes.shape
    capacity = min(tok_rows, 2 * tok_rows * top_count // experts)
    gate_w, up_w = w_gate[0], w_up[0]
    if tok_rows * owners <= experts * capacity and owners % CORES == 0:
        gram_local = gather_grams(tokens, routes, gate_w, up_w)
    else:
        gram_local = packed_grams(tokens, routes, gate_w, up_w, capacity)
    rows_mean = data_ranks * tok_rows * top_count
    return finish(gram_local, rows_mean, data_ranks, factor_width)


def over_lanes(column, width):
    return jnp.concatenate([column] * (width // column.shape[1]), axis=1)


def factor_panel(x, columns, sublane):
    rows, width = x.shape
    factor = jnp.zeros_like(x)
    for k in range(rows):
        scale = lax.rsqrt(jnp.broadcast_to(columns[k][k : k + 1, :], columns[k].shape))
        lower = columns[k] * scale
        upper = jnp.broadcast_to(x[k : k + 1, :], x.shape) * over_lanes(scale, width)
        factor = jnp.where(sublane == k, upper, factor)
        for j in range(k + 1, rows):
            columns[j] = columns[j] - lower * jnp.broadcast_to(lower[j : j + 1, :], lower.shape)
        if k + 1 < rows:
            x = x - over_lanes(lower, width) * upper
    return factor


def outer_sum(a, b):
    return lax.dot_general(
        a, b, (((0,), (0,)), ((), ())), precision=lax.Precision.HIGHEST, preferred_element_type=jnp.float32
    )


def factor_kernel(mine_ref, theirs_ref, out_ref, rest_ref, *, rows_mean):
    size = mine_ref.shape[0]
    block, panel = 128, 8
    row = lax.broadcasted_iota(jnp.int32, (size, size), 0)
    col = lax.broadcasted_iota(jnp.int32, (size, size), 1)
    rest_ref[...] = (mine_ref[...] + theirs_ref[...]) / rows_mean + jnp.where(row == col, RIDGE, 0.0)
    for base in range(0, size, block):
        width = size - base
        end = base + block
        if base:
            out_ref[base:end, :base] = jnp.zeros((block, base), jnp.float32)
        sublane = lax.broadcasted_iota(jnp.int32, (panel, width), 0)
        lane = lax.broadcasted_iota(jnp.int32, (panel, width), 1)

        def step(p, carry):
            first = panel * p
            rows = pl.ds(pl.multiple_of(base + first, panel), panel)
            x = rest_ref[rows, base:]
            corner = x[:, :block]
            columns = [
                jnp.take_along_axis(
                    corner, jnp.full(corner.shape, first + j, jnp.int32), axis=1, mode="promise_in_bounds"
                )
                for j in range(panel)
            ]
            factor = factor_panel(x, columns, sublane)
            out_ref[rows, base:] = jnp.where(lane >= sublane + first, factor, 0.0)
            below = jnp.where(lane[:, :block] >= first + panel, factor[:, :block], 0.0)
            rest_ref[base:end, base:] -= outer_sum(below, factor)
            return carry

        lax.fori_loop(0, block // panel, step, 0)
        if end < size:
            done = out_ref[base:end, end:]
            rest_ref[end:, end:] -= outer_sum(done, done)


def factor_of(mine, theirs, rows_mean):
    size = mine.shape[0]
    return pl.pallas_call(
        functools.partial(factor_kernel, rows_mean=rows_mean),
        in_specs=[pl.BlockSpec(memory_space=pltpu.VMEM)] * 2,
        out_specs=pl.BlockSpec(memory_space=pltpu.VMEM),
        out_shape=jax.ShapeDtypeStruct((size, size), jnp.float32),
        scratch_shapes=[pltpu.VMEM((size, size), jnp.float32)],
        name="factor",
    )(mine, theirs)


def finish(gram_local, rows_mean, data_ranks, factor_width):
    block_rows = factor_width // data_ranks
    my_rank = lax.axis_index("dp")
    theirs = jnp.zeros_like(gram_local)
    for s in range(1, data_ranks):
        moved = lax.ppermute(gram_local, "dp", [(r, (r + s) % data_ranks) for r in range(data_ranks)])
        theirs = moved if s == 1 else theirs + moved
    factor = factor_of(gram_local, theirs, rows_mean)
    my_rows = lax.dynamic_slice_in_dim(factor, my_rank * block_rows, block_rows, 0)
    return my_rows.reshape(1, block_rows, factor_width)


def solution(mesh):
    in_specs = (
        P(("groups", "dp", "expert"), None),
        P(("groups", "dp", "expert"), None),
        P(("groups", "expert"), None, None),
        P(("groups", "expert"), None, None),
    )
    out_specs = P(("groups", "expert"), "dp", None)
    return jax.shard_map(body, mesh=mesh, in_specs=in_specs, out_specs=out_specs, check_vma=False)
```

```python
import functools

import jax
import jax.numpy as jnp
from jax import lax
from jax.experimental import pallas as pl
from jax.experimental.pallas import tpu as pltpu
from jax.sharding import PartitionSpec as P


RIDGE = 0.05
CORES = 2
CHIPS_DENSE = 4


def hidden_gram_kernel(me_ref, own_ref, other_ref, own_names_ref, other_names_ref, gate_ref, up_ref, *rest, slot):
    gram_ref, hidden_ref = rest[-2:]
    hw = gate_ref.shape[1]
    width = 256
    top = own_names_ref.shape[0] // CHIPS_DENSE
    mine = slice(slot * top, (slot + 1) * top)
    named = jnp.concatenate([own_names_ref[mine, :], other_names_ref[mine, :]], axis=0) == me_ref[0]
    named = named.astype(jnp.float32).T
    member = jnp.concatenate(
        [jnp.max(named[:, c * top : (c + 1) * top], axis=1, keepdims=True) for c in range(CORES)], axis=0
    )
    x = jnp.concatenate([own_ref[...], other_ref[...]], axis=0)

    def step(i, carry):
        at = pl.ds(pl.multiple_of(i * width, width), width)
        gate = jnp.dot(x, gate_ref[:, at], preferred_element_type=jnp.float32)
        up = jnp.dot(x, up_ref[:, at], preferred_element_type=jnp.float32)
        value = gate / (1.0 + jnp.exp(-gate)) * up
        hidden_ref[:, at] = jnp.where(member > 0, value, 0.0).astype(jnp.bfloat16)
        return carry

    lax.fori_loop(0, hw // width, step, 0)
    h = hidden_ref[...]
    gram = lax.dot_general(h, h, (((0,), (0,)), ((), ())), preferred_element_type=jnp.float32)
    gram_ref[...] = gram if len(rest) == 2 else rest[0][...] + gram


def hidden_gram(me, own, other, own_names, other_names, slot, gate_w, up_w, gram=None):
    rows, model = own.shape
    hw = gate_w.shape[1]
    args = [me, own, other, own_names, other_names, gate_w, up_w]
    in_specs = [pl.BlockSpec(memory_space=pltpu.SMEM)] + [pl.BlockSpec(memory_space=pltpu.VMEM)] * 6
    aliases = {}
    if gram is not None:
        in_specs.append(pl.BlockSpec(memory_space=pltpu.VMEM))
        args.append(gram)
        aliases = {7: 0}
    return pl.pallas_call(
        functools.partial(hidden_gram_kernel, slot=slot),
        in_specs=in_specs,
        out_specs=pl.BlockSpec(memory_space=pltpu.VMEM),
        out_shape=jax.ShapeDtypeStruct((hw, hw), jnp.float32),
        scratch_shapes=[pltpu.VMEM((CORES * rows, hw), jnp.bfloat16)],
        input_output_aliases=aliases,
        compiler_params=pltpu.CompilerParams(vmem_limit_bytes=24 << 20),
        cost_estimate=pl.CostEstimate(
            flops=2 * CORES * rows * model * 2 * hw + 2 * CORES * rows * hw * hw,
            bytes_accessed=2 * (CORES * rows * model + 2 * model * hw) + 4 * hw * hw,
            transcendentals=CORES * rows * hw,
        ),
    )(*args)


def between_chips(pairs):
    return [(s * CORES + c, d * CORES + c) for s, d in pairs for c in range(CORES)]


def gather_grams(tokens, routes, gate_w, up_w):
    me = lax.axis_index("expert")
    move = lambda x, pairs: lax.ppermute(x, "expert", between_chips(pairs))
    swap = lambda x: lax.ppermute(x, "expert", [(e, e ^ 1) for e in range(CHIPS_DENSE * CORES)])
    near = [(z, z ^ 1) for z in range(CHIPS_DENSE)]
    cross = [(z, z ^ 3) for z in range(CHIPS_DENSE)]
    two = [(z, z ^ 2) for z in range(CHIPS_DENSE)]

    names = routes.T
    first = move(tokens, near)
    named = [names]
    for pairs in [near, cross, two]:
        named.append(move(names, pairs))
    own_names = jnp.concatenate(named, axis=0)
    other_names = swap(own_names)
    second = move(tokens, cross)
    far = move(tokens, [(0, 2), (3, 1)])
    onward = move(second, [(1, 0), (2, 3)])
    third = far + onward

    me = me.astype(jnp.int32).reshape(1)
    gram = None
    for slot, own in enumerate([tokens, first, second, third]):
        other = swap(own)
        gram = hidden_gram(me, own, other, own_names, other_names, slot, gate_w, up_w, gram)
    return gram


def packed_grams(tokens, routes, gate_w, up_w, capacity):
    owners = lax.axis_size("expert")
    experts = owners
    model_width = tokens.shape[1]
    tok_rows, top_count = routes.shape
    assigned = routes.reshape(-1)
    onehot = (assigned[:, None] == jnp.arange(experts, dtype=jnp.int32)[None, :]).astype(jnp.int32)
    position = jnp.sum(jnp.cumsum(onehot, axis=0) * onehot, axis=1) - 1
    target = assigned * capacity + position
    anchor = jnp.arange(tok_rows * top_count, dtype=jnp.int32) // top_count
    source_row = jnp.zeros((experts * capacity,), jnp.int32).at[target].set(anchor)
    filled = jnp.zeros((experts * capacity,), jnp.int32).at[target].set(1)
    outbox = jnp.where(filled[:, None] > 0, tokens[source_row], jnp.zeros((), tokens.dtype))
    outbox = outbox.reshape(experts, capacity, model_width)
    arrived = lax.all_to_all(outbox, "expert", split_axis=0, concat_axis=0, tiled=True)
    flattened = arrived.reshape(-1, model_width)
    gate_proj = jnp.dot(flattened, gate_w, preferred_element_type=jnp.float32)
    up_proj = jnp.dot(flattened, up_w, preferred_element_type=jnp.float32)
    hidden = (jax.nn.silu(gate_proj) * up_proj).astype(jnp.bfloat16)
    return lax.dot_general(hidden, hidden, (((0,), (0,)), ((), ())), preferred_element_type=jnp.float32)


def body(tokens, routes, w_gate, w_up):
    owners = lax.axis_size("expert")
    data_ranks = lax.axis_size("dp")
    experts = w_gate.shape[0] * owners
    factor_width = w_gate.shape[2]
    tok_rows, top_count = routes.shape
    capacity = min(tok_rows, 2 * tok_rows * top_count // experts)
    gate_w, up_w = w_gate[0], w_up[0]
    if tok_rows * owners <= experts * capacity and owners == CHIPS_DENSE * CORES:
        gram_local = gather_grams(tokens, routes, gate_w, up_w)
    else:
        gram_local = packed_grams(tokens, routes, gate_w, up_w, capacity)
    rows_mean = data_ranks * tok_rows * top_count
    return finish(gram_local, rows_mean, data_ranks, factor_width)


def over_lanes(column, width):
    return jnp.concatenate([column] * (width // column.shape[1]), axis=1)


def factor_panel(x, columns, sublane):
    rows, width = x.shape
    factor = jnp.zeros_like(x)
    for k in range(rows):
        scale = lax.rsqrt(jnp.broadcast_to(columns[k][k : k + 1, :], columns[k].shape))
        lower = columns[k] * scale
        upper = jnp.broadcast_to(x[k : k + 1, :], x.shape) * over_lanes(scale, width)
        factor = jnp.where(sublane == k, upper, factor)
        for j in range(k + 1, rows):
            columns[j] = columns[j] - lower * jnp.broadcast_to(lower[j : j + 1, :], lower.shape)
        if k + 1 < rows:
            x = x - over_lanes(lower, width) * upper
    return factor


def outer_sum(a, b):
    return lax.dot_general(
        a, b, (((0,), (0,)), ((), ())), precision=lax.Precision.HIGHEST, preferred_element_type=jnp.float32
    )


def factor_kernel(mine_ref, theirs_ref, out_ref, rest_ref, *, rows_mean):
    size = mine_ref.shape[0]
    block, panel = 128, 8
    row = lax.broadcasted_iota(jnp.int32, (size, size), 0)
    col = lax.broadcasted_iota(jnp.int32, (size, size), 1)
    rest_ref[...] = (mine_ref[...] + theirs_ref[...]) / rows_mean + jnp.where(row == col, RIDGE, 0.0)
    for base in range(0, size, block):
        width = size - base
        end = base + block
        if base:
            out_ref[base:end, :base] = jnp.zeros((block, base), jnp.float32)
        sublane = lax.broadcasted_iota(jnp.int32, (panel, width), 0)
        lane = lax.broadcasted_iota(jnp.int32, (panel, width), 1)

        def step(p, carry):
            first = panel * p
            rows = pl.ds(pl.multiple_of(base + first, panel), panel)
            x = rest_ref[rows, base:]
            corner = x[:, :block]
            columns = [
                jnp.take_along_axis(
                    corner, jnp.full(corner.shape, first + j, jnp.int32), axis=1, mode="promise_in_bounds"
                )
                for j in range(panel)
            ]
            factor = factor_panel(x, columns, sublane)
            out_ref[rows, base:] = jnp.where(lane >= sublane + first, factor, 0.0)
            below = jnp.where(lane[:, :block] >= first + panel, factor[:, :block], 0.0)
            rest_ref[base:end, base:] -= outer_sum(below, factor)
            return carry

        lax.fori_loop(0, block // panel, step, 0)
        if end < size:
            done = out_ref[base:end, end:]
            rest_ref[end:, end:] -= outer_sum(done, done)


def factor_of(mine, theirs, rows_mean):
    size = mine.shape[0]
    return pl.pallas_call(
        functools.partial(factor_kernel, rows_mean=rows_mean),
        in_specs=[pl.BlockSpec(memory_space=pltpu.VMEM)] * 2,
        out_specs=pl.BlockSpec(memory_space=pltpu.VMEM),
        out_shape=jax.ShapeDtypeStruct((size, size), jnp.float32),
        scratch_shapes=[pltpu.VMEM((size, size), jnp.float32)],
        name="factor",
    )(mine, theirs)


def finish(gram_local, rows_mean, data_ranks, factor_width):
    block_rows = factor_width // data_ranks
    my_rank = lax.axis_index("dp")
    theirs = jnp.zeros_like(gram_local)
    for s in range(1, data_ranks):
        moved = lax.ppermute(gram_local, "dp", [(r, (r + s) % data_ranks) for r in range(data_ranks)])
        theirs = moved if s == 1 else theirs + moved
    factor = factor_of(gram_local, theirs, rows_mean)
    my_rows = lax.dynamic_slice_in_dim(factor, my_rank * block_rows, block_rows, 0)
    return my_rows.reshape(1, block_rows, factor_width)


def solution(mesh):
    in_specs = (
        P(("groups", "dp", "expert"), None),
        P(("groups", "dp", "expert"), None),
        P(("groups", "expert"), None, None),
        P(("groups", "expert"), None, None),
    )
    out_specs = P(("groups", "expert"), "dp", None)
    return jax.shard_map(body, mesh=mesh, in_specs=in_specs, out_specs=out_specs, check_vma=False)
```

```python
import functools

import jax
import jax.numpy as jnp
from jax import lax
from jax.experimental import pallas as pl
from jax.experimental.pallas import tpu as pltpu
from jax.sharding import PartitionSpec as P


RIDGE = 0.05
CORES = 2
CHIPS_DENSE = 4


def hidden_kernel(me_ref, own_ref, other_ref, own_names_ref, other_names_ref, gate_ref, up_ref, hidden_ref, *, at, top):
    hw = gate_ref.shape[1]
    width = 256
    mine = slice(at * top, (at + 1) * top)
    named = jnp.concatenate([own_names_ref[mine, :], other_names_ref[mine, :]], axis=0) == me_ref[0]
    named = named.astype(jnp.float32).T
    member = jnp.concatenate(
        [jnp.max(named[:, c * top : (c + 1) * top], axis=1, keepdims=True) for c in range(CORES)], axis=0
    )
    x = jnp.concatenate([own_ref[...], other_ref[...]], axis=0)

    def step(i, carry):
        columns = pl.ds(pl.multiple_of(i * width, width), width)
        gate = jnp.dot(x, gate_ref[:, columns], preferred_element_type=jnp.float32)
        up = jnp.dot(x, up_ref[:, columns], preferred_element_type=jnp.float32)
        value = gate / (1.0 + jnp.exp(-gate)) * up
        hidden_ref[:, columns] = jnp.where(member > 0, value, 0.0).astype(jnp.bfloat16)
        return carry

    lax.fori_loop(0, hw // width, step, 0)


def hidden_of(me, own, other, own_names, other_names, at, top, gate_w, up_w):
    rows, model = own.shape
    hw = gate_w.shape[1]
    return pl.pallas_call(
        functools.partial(hidden_kernel, at=at, top=top),
        in_specs=[pl.BlockSpec(memory_space=pltpu.SMEM)] + [pl.BlockSpec(memory_space=pltpu.VMEM)] * 6,
        out_specs=pl.BlockSpec(memory_space=pltpu.VMEM),
        out_shape=jax.ShapeDtypeStruct((CORES * rows, hw), jnp.bfloat16),
        compiler_params=pltpu.CompilerParams(vmem_limit_bytes=24 << 20),
        cost_estimate=pl.CostEstimate(
            flops=2 * CORES * rows * model * 2 * hw,
            bytes_accessed=2 * (CORES * rows * model + 2 * model * hw) + 2 * CORES * rows * hw,
            transcendentals=CORES * rows * hw,
        ),
        name="hidden",
    )(me, own, other, own_names, other_names, gate_w, up_w)


def gram_of(refs):
    total = None
    for ref in refs:
        h = ref[...]
        part = lax.dot_general(h, h, (((0,), (0,)), ((), ())), preferred_element_type=jnp.float32)
        total = part if total is None else total + part
    return total


def gram_kernel(*refs):
    refs[-1][...] = gram_of(refs[:-1])


def partial_gram(hiddens):
    rows, hw = hiddens[0].shape
    return pl.pallas_call(
        gram_kernel,
        in_specs=[pl.BlockSpec(memory_space=pltpu.VMEM)] * len(hiddens),
        out_specs=pl.BlockSpec(memory_space=pltpu.VMEM),
        out_shape=jax.ShapeDtypeStruct((hw, hw), jnp.float32),
        compiler_params=pltpu.CompilerParams(vmem_limit_bytes=24 << 20),
        cost_estimate=pl.CostEstimate(
            flops=2 * len(hiddens) * rows * hw * hw,
            bytes_accessed=2 * len(hiddens) * rows * hw + 4 * hw * hw,
            transcendentals=0,
        ),
        name="partial_gram",
    )(*hiddens)


def between_chips(pairs):
    return [(s * CORES + c, d * CORES + c) for s, d in pairs for c in range(CORES)]


def gathered(tokens, routes, gate_w, up_w):
    me = lax.axis_index("expert").astype(jnp.int32).reshape(1)
    data_ranks = lax.axis_size("dp")
    top = routes.shape[1]
    move = lambda x, pairs: lax.ppermute(x, "expert", between_chips(pairs))
    swap = lambda x: lax.ppermute(x, "expert", [(e, e ^ 1) for e in range(CHIPS_DENSE * CORES)])
    turn = lambda x, s: lax.ppermute(x, "dp", [(r, (r + s) % data_ranks) for r in range(data_ranks)])
    near = [(z, z ^ 1) for z in range(CHIPS_DENSE)]
    cross = [(z, z ^ 3) for z in range(CHIPS_DENSE)]
    two = [(z, z ^ 2) for z in range(CHIPS_DENSE)]

    names = routes.T
    first = move(tokens, near)
    second = move(tokens, cross)
    far = move(tokens, [(0, 2), (3, 1)])
    onward = move(second, [(1, 0), (2, 3)])
    moved = []
    for pairs in [near, cross, two]:
        moved.append(move(names, pairs))
    moved = jnp.concatenate(moved, axis=0)
    other_names = swap(names)
    other_moved = swap(moved)

    hiddens = []
    for slot, own in enumerate([tokens, first, second, far + onward]):
        other = swap(own)
        if slot == 0:
            hidden = hidden_of(me, own, other, names, other_names, 0, top, gate_w, up_w)
        else:
            hidden = hidden_of(me, own, other, moved, other_moved, slot - 1, top, gate_w, up_w)
        hiddens.append([hidden] + [turn(hidden, s) for s in range(1, data_ranks)])
    early = partial_gram(sum(hiddens[:-1], []))
    return early, hiddens[-1]


def packed_grams(tokens, routes, gate_w, up_w, capacity):
    owners = lax.axis_size("expert")
    experts = owners
    model_width = tokens.shape[1]
    tok_rows, top_count = routes.shape
    assigned = routes.reshape(-1)
    onehot = (assigned[:, None] == jnp.arange(experts, dtype=jnp.int32)[None, :]).astype(jnp.int32)
    position = jnp.sum(jnp.cumsum(onehot, axis=0) * onehot, axis=1) - 1
    target = assigned * capacity + position
    anchor = jnp.arange(tok_rows * top_count, dtype=jnp.int32) // top_count
    source_row = jnp.zeros((experts * capacity,), jnp.int32).at[target].set(anchor)
    filled = jnp.zeros((experts * capacity,), jnp.int32).at[target].set(1)
    outbox = jnp.where(filled[:, None] > 0, tokens[source_row], jnp.zeros((), tokens.dtype))
    outbox = outbox.reshape(experts, capacity, model_width)
    arrived = lax.all_to_all(outbox, "expert", split_axis=0, concat_axis=0, tiled=True)
    flattened = arrived.reshape(-1, model_width)
    gate_proj = jnp.dot(flattened, gate_w, preferred_element_type=jnp.float32)
    up_proj = jnp.dot(flattened, up_w, preferred_element_type=jnp.float32)
    hidden = (jax.nn.silu(gate_proj) * up_proj).astype(jnp.bfloat16)
    return lax.dot_general(hidden, hidden, (((0,), (0,)), ((), ())), preferred_element_type=jnp.float32)


def body(tokens, routes, w_gate, w_up):
    owners = lax.axis_size("expert")
    data_ranks = lax.axis_size("dp")
    experts = w_gate.shape[0] * owners
    tok_rows, top_count = routes.shape
    capacity = min(tok_rows, 2 * tok_rows * top_count // experts)
    gate_w, up_w = w_gate[0], w_up[0]
    if tok_rows * owners <= experts * capacity and owners == CHIPS_DENSE * CORES:
        early, late = gathered(tokens, routes, gate_w, up_w)
    else:
        gram = packed_grams(tokens, routes, gate_w, up_w, capacity)
        early, late = gram, []
        for s in range(1, data_ranks):
            early = early + lax.ppermute(gram, "dp", [(r, (r + s) % data_ranks) for r in range(data_ranks)])
    rows_mean = data_ranks * tok_rows * top_count
    return factor_rows(early, late, rows_mean, data_ranks)[None]


def over_lanes(column, width):
    return jnp.concatenate([column] * (width // column.shape[1]), axis=1)


def factor_panel(x, columns, sublane):
    rows, width = x.shape
    factor = jnp.zeros_like(x)
    for k in range(rows):
        scale = lax.rsqrt(jnp.broadcast_to(columns[k][k : k + 1, :], columns[k].shape))
        lower = columns[k] * scale
        upper = jnp.broadcast_to(x[k : k + 1, :], x.shape) * over_lanes(scale, width)
        factor = jnp.where(sublane == k, upper, factor)
        for j in range(k + 1, rows):
            columns[j] = columns[j] - lower * jnp.broadcast_to(lower[j : j + 1, :], lower.shape)
        if k + 1 < rows:
            x = x - over_lanes(lower, width) * upper
    return factor


def outer_sum(a, b):
    return lax.dot_general(
        a, b, (((0,), (0,)), ((), ())), precision=lax.Precision.HIGHEST, preferred_element_type=jnp.float32
    )


def factor_kernel(rank_ref, early_ref, *refs, rows_mean):
    late_refs, (my_rows_ref, out_ref, rest_ref) = refs[:-3], refs[-3:]
    size = early_ref.shape[0]
    block, panel = 128, 8
    row = lax.broadcasted_iota(jnp.int32, (size, size), 0)
    col = lax.broadcasted_iota(jnp.int32, (size, size), 1)
    gram = early_ref[...]
    if late_refs:
        gram = gram + gram_of(late_refs)
    rest_ref[...] = gram / rows_mean + jnp.where(row == col, RIDGE, 0.0)
    for base in range(0, size, block):
        width = size - base
        end = base + block
        if base:
            out_ref[base:end, :base] = jnp.zeros((block, base), jnp.float32)
        sublane = lax.broadcasted_iota(jnp.int32, (panel, width), 0)
        lane = lax.broadcasted_iota(jnp.int32, (panel, width), 1)

        def step(p, carry):
            first = panel * p
            rows = pl.ds(pl.multiple_of(base + first, panel), panel)
            x = rest_ref[rows, base:]
            corner = x[:, :block]
            columns = [
                jnp.take_along_axis(
                    corner, jnp.full(corner.shape, first + j, jnp.int32), axis=1, mode="promise_in_bounds"
                )
                for j in range(panel)
            ]
            factor = factor_panel(x, columns, sublane)
            out_ref[rows, base:] = jnp.where(lane >= sublane + first, factor, 0.0)
            below = jnp.where(lane[:, :block] >= first + panel, factor[:, :block], 0.0)
            rest_ref[base:end, base:] -= outer_sum(below, factor)
            return carry

        lax.fori_loop(0, block // panel, step, 0)
        if end < size:
            done = out_ref[base:end, end:]
            rest_ref[end:, end:] -= outer_sum(done, done)
    count = my_rows_ref.shape[0]
    my_rows_ref[...] = out_ref[pl.ds(pl.multiple_of(rank_ref[0] * count, count), count), :]


def factor_rows(early, late, rows_mean, data_ranks):
    size = early.shape[0]
    rank = lax.axis_index("dp").astype(jnp.int32).reshape(1)
    return pl.pallas_call(
        functools.partial(factor_kernel, rows_mean=rows_mean),
        in_specs=[pl.BlockSpec(memory_space=pltpu.SMEM)] + [pl.BlockSpec(memory_space=pltpu.VMEM)] * (1 + len(late)),
        out_specs=pl.BlockSpec(memory_space=pltpu.VMEM),
        out_shape=jax.ShapeDtypeStruct((size // data_ranks, size), jnp.float32),
        scratch_shapes=[pltpu.VMEM((size, size), jnp.float32)] * 2,
        compiler_params=pltpu.CompilerParams(vmem_limit_bytes=24 << 20),
        name="factor",
    )(rank, early, *late)


def solution(mesh):
    in_specs = (
        P(("groups", "dp", "expert"), None),
        P(("groups", "dp", "expert"), None),
        P(("groups", "expert"), None, None),
        P(("groups", "expert"), None, None),
    )
    out_specs = P(("groups", "expert"), "dp", None)
    return jax.shard_map(body, mesh=mesh, in_specs=in_specs, out_specs=out_specs, check_vma=False)
```

```python
import functools

import jax
import jax.numpy as jnp
from jax import lax
from jax.experimental import pallas as pl
from jax.experimental.pallas import tpu as pltpu
from jax.sharding import PartitionSpec as P


RIDGE = 0.05
CORES = 2
CHIPS_DENSE = 4


def hidden_kernel(me_ref, own_ref, other_ref, own_names_ref, other_names_ref, gate_ref, up_ref, hidden_ref, *, at, top):
    hw = gate_ref.shape[1]
    width = 256
    mine = slice(at * top, (at + 1) * top)
    named = jnp.concatenate([own_names_ref[mine, :], other_names_ref[mine, :]], axis=0) == me_ref[0]
    named = named.astype(jnp.float32).T
    member = jnp.concatenate(
        [jnp.max(named[:, c * top : (c + 1) * top], axis=1, keepdims=True) for c in range(CORES)], axis=0
    )
    x = jnp.concatenate([own_ref[...], other_ref[...]], axis=0)

    def step(i, carry):
        columns = pl.ds(pl.multiple_of(i * width, width), width)
        gate = jnp.dot(x, gate_ref[:, columns], preferred_element_type=jnp.float32)
        up = jnp.dot(x, up_ref[:, columns], preferred_element_type=jnp.float32)
        value = gate / (1.0 + jnp.exp(-gate)) * up
        hidden_ref[:, columns] = jnp.where(member > 0, value, 0.0).astype(jnp.bfloat16)
        return carry

    lax.fori_loop(0, hw // width, step, 0)


def hidden_of(me, own, other, own_names, other_names, at, top, gate_w, up_w):
    rows, model = own.shape
    hw = gate_w.shape[1]
    return pl.pallas_call(
        functools.partial(hidden_kernel, at=at, top=top),
        in_specs=[pl.BlockSpec(memory_space=pltpu.SMEM)] + [pl.BlockSpec(memory_space=pltpu.VMEM)] * 6,
        out_specs=pl.BlockSpec(memory_space=pltpu.VMEM),
        out_shape=jax.ShapeDtypeStruct((CORES * rows, hw), jnp.bfloat16),
        compiler_params=pltpu.CompilerParams(vmem_limit_bytes=24 << 20),
        cost_estimate=pl.CostEstimate(
            flops=2 * CORES * rows * model * 2 * hw,
            bytes_accessed=2 * (CORES * rows * model + 2 * model * hw) + 2 * CORES * rows * hw,
            transcendentals=CORES * rows * hw,
        ),
        name="hidden",
    )(me, own, other, own_names, other_names, gate_w, up_w)


def gram_of(refs):
    total = None
    for ref in refs:
        h = ref[...]
        part = lax.dot_general(h, h, (((0,), (0,)), ((), ())), preferred_element_type=jnp.float32)
        total = part if total is None else total + part
    return total


def gram_kernel(*refs):
    refs[-1][...] = gram_of(refs[:-1])


def partial_gram(hiddens):
    rows, hw = hiddens[0].shape
    return pl.pallas_call(
        gram_kernel,
        in_specs=[pl.BlockSpec(memory_space=pltpu.VMEM)] * len(hiddens),
        out_specs=pl.BlockSpec(memory_space=pltpu.VMEM),
        out_shape=jax.ShapeDtypeStruct((hw, hw), jnp.float32),
        compiler_params=pltpu.CompilerParams(vmem_limit_bytes=24 << 20),
        cost_estimate=pl.CostEstimate(
            flops=2 * len(hiddens) * rows * hw * hw,
            bytes_accessed=2 * len(hiddens) * rows * hw + 4 * hw * hw,
            transcendentals=0,
        ),
        name="partial_gram",
    )(*hiddens)


def between_chips(pairs):
    return [(s * CORES + c, d * CORES + c) for s, d in pairs for c in range(CORES)]


def gathered(tokens, routes, gate_w, up_w):
    me = lax.axis_index("expert").astype(jnp.int32).reshape(1)
    data_ranks = lax.axis_size("dp")
    top = routes.shape[1]
    move = lambda x, pairs: lax.ppermute(x, "expert", between_chips(pairs))
    swap = lambda x: lax.ppermute(x, "expert", [(e, e ^ 1) for e in range(CHIPS_DENSE * CORES)])
    turn = lambda x, s: lax.ppermute(x, "dp", [(r, (r + s) % data_ranks) for r in range(data_ranks)])
    ring = lambda s: [(z, (z + s) % CHIPS_DENSE) for z in range(CHIPS_DENSE)]

    names = routes.T
    below = move(tokens, ring(1))
    above = move(tokens, ring(-1))
    far = move(tokens, [(0, 2), (3, 1)])
    on_up = move(below, [(2, 3)])
    on_down = move(above, [(1, 0)])
    moved = []
    for pairs in [ring(1), ring(-1), ring(2)]:
        moved.append(move(names, pairs))
    moved = jnp.concatenate(moved, axis=0)
    other_names = swap(names)
    other_moved = swap(moved)

    hiddens = []
    for slot, own in enumerate([tokens, below, above, far + on_up + on_down]):
        other = swap(own)
        if slot == 0:
            hidden = hidden_of(me, own, other, names, other_names, 0, top, gate_w, up_w)
        else:
            hidden = hidden_of(me, own, other, moved, other_moved, slot - 1, top, gate_w, up_w)
        hiddens.append([hidden] + [turn(hidden, s) for s in range(1, data_ranks)])
    early = partial_gram(sum(hiddens[:-1], []))
    return early, hiddens[-1]


def packed_grams(tokens, routes, gate_w, up_w, capacity):
    owners = lax.axis_size("expert")
    experts = owners
    model_width = tokens.shape[1]
    tok_rows, top_count = routes.shape
    assigned = routes.reshape(-1)
    onehot = (assigned[:, None] == jnp.arange(experts, dtype=jnp.int32)[None, :]).astype(jnp.int32)
    position = jnp.sum(jnp.cumsum(onehot, axis=0) * onehot, axis=1) - 1
    target = assigned * capacity + position
    anchor = jnp.arange(tok_rows * top_count, dtype=jnp.int32) // top_count
    source_row = jnp.zeros((experts * capacity,), jnp.int32).at[target].set(anchor)
    filled = jnp.zeros((experts * capacity,), jnp.int32).at[target].set(1)
    outbox = jnp.where(filled[:, None] > 0, tokens[source_row], jnp.zeros((), tokens.dtype))
    outbox = outbox.reshape(experts, capacity, model_width)
    arrived = lax.all_to_all(outbox, "expert", split_axis=0, concat_axis=0, tiled=True)
    flattened = arrived.reshape(-1, model_width)
    gate_proj = jnp.dot(flattened, gate_w, preferred_element_type=jnp.float32)
    up_proj = jnp.dot(flattened, up_w, preferred_element_type=jnp.float32)
    hidden = (jax.nn.silu(gate_proj) * up_proj).astype(jnp.bfloat16)
    return lax.dot_general(hidden, hidden, (((0,), (0,)), ((), ())), preferred_element_type=jnp.float32)


def body(tokens, routes, w_gate, w_up):
    owners = lax.axis_size("expert")
    data_ranks = lax.axis_size("dp")
    experts = w_gate.shape[0] * owners
    tok_rows, top_count = routes.shape
    capacity = min(tok_rows, 2 * tok_rows * top_count // experts)
    gate_w, up_w = w_gate[0], w_up[0]
    if tok_rows * owners <= experts * capacity and owners == CHIPS_DENSE * CORES:
        early, late = gathered(tokens, routes, gate_w, up_w)
    else:
        gram = packed_grams(tokens, routes, gate_w, up_w, capacity)
        early, late = gram, []
        for s in range(1, data_ranks):
            early = early + lax.ppermute(gram, "dp", [(r, (r + s) % data_ranks) for r in range(data_ranks)])
    rows_mean = data_ranks * tok_rows * top_count
    return factor_rows(early, late, rows_mean, data_ranks)[None]


def over_lanes(column, width):
    return jnp.concatenate([column] * (width // column.shape[1]), axis=1)


def factor_panel(x, columns, sublane):
    rows, width = x.shape
    factor = jnp.zeros_like(x)
    for k in range(rows):
        scale = lax.rsqrt(jnp.broadcast_to(columns[k][k : k + 1, :], columns[k].shape))
        lower = columns[k] * scale
        upper = jnp.broadcast_to(x[k : k + 1, :], x.shape) * over_lanes(scale, width)
        factor = jnp.where(sublane == k, upper, factor)
        for j in range(k + 1, rows):
            columns[j] = columns[j] - lower * jnp.broadcast_to(lower[j : j + 1, :], lower.shape)
        if k + 1 < rows:
            x = x - over_lanes(lower, width) * upper
    return factor


def outer_sum(a, b):
    return lax.dot_general(
        a, b, (((0,), (0,)), ((), ())), precision=lax.Precision.HIGHEST, preferred_element_type=jnp.float32
    )


def factor_kernel(rank_ref, early_ref, *refs, rows_mean):
    late_refs, (my_rows_ref, out_ref, rest_ref) = refs[:-3], refs[-3:]
    size = early_ref.shape[0]
    block, panel = 128, 8
    row = lax.broadcasted_iota(jnp.int32, (size, size), 0)
    col = lax.broadcasted_iota(jnp.int32, (size, size), 1)
    gram = early_ref[...]
    if late_refs:
        gram = gram + gram_of(late_refs)
    rest_ref[...] = gram / rows_mean + jnp.where(row == col, RIDGE, 0.0)
    for base in range(0, size, block):
        width = size - base
        end = base + block
        if base:
            out_ref[base:end, :base] = jnp.zeros((block, base), jnp.float32)
        sublane = lax.broadcasted_iota(jnp.int32, (panel, width), 0)
        lane = lax.broadcasted_iota(jnp.int32, (panel, width), 1)

        def step(p, carry):
            first = panel * p
            rows = pl.ds(pl.multiple_of(base + first, panel), panel)
            x = rest_ref[rows, base:]
            corner = x[:, :block]
            columns = [
                jnp.take_along_axis(
                    corner, jnp.full(corner.shape, first + j, jnp.int32), axis=1, mode="promise_in_bounds"
                )
                for j in range(panel)
            ]
            factor = factor_panel(x, columns, sublane)
            out_ref[rows, base:] = jnp.where(lane >= sublane + first, factor, 0.0)
            below = jnp.where(lane[:, :block] >= first + panel, factor[:, :block], 0.0)
            rest_ref[base:end, base:] -= outer_sum(below, factor)
            return carry

        lax.fori_loop(0, block // panel, step, 0)
        if end < size:
            done = out_ref[base:end, end:]
            rest_ref[end:, end:] -= outer_sum(done, done)
    count = my_rows_ref.shape[0]
    my_rows_ref[...] = out_ref[pl.ds(pl.multiple_of(rank_ref[0] * count, count), count), :]


def factor_rows(early, late, rows_mean, data_ranks):
    size = early.shape[0]
    rank = lax.axis_index("dp").astype(jnp.int32).reshape(1)
    return pl.pallas_call(
        functools.partial(factor_kernel, rows_mean=rows_mean),
        in_specs=[pl.BlockSpec(memory_space=pltpu.SMEM)] + [pl.BlockSpec(memory_space=pltpu.VMEM)] * (1 + len(late)),
        out_specs=pl.BlockSpec(memory_space=pltpu.VMEM),
        out_shape=jax.ShapeDtypeStruct((size // data_ranks, size), jnp.float32),
        scratch_shapes=[pltpu.VMEM((size, size), jnp.float32)] * 2,
        compiler_params=pltpu.CompilerParams(vmem_limit_bytes=24 << 20),
        name="factor",
    )(rank, early, *late)


def solution(mesh):
    in_specs = (
        P(("groups", "dp", "expert"), None),
        P(("groups", "dp", "expert"), None),
        P(("groups", "expert"), None, None),
        P(("groups", "expert"), None, None),
    )
    out_specs = P(("groups", "expert"), "dp", None)
    return jax.shard_map(body, mesh=mesh, in_specs=in_specs, out_specs=out_specs, check_vma=False)
```

```python
import functools

import jax
import jax.numpy as jnp
from jax import lax
from jax.experimental import pallas as pl
from jax.experimental.pallas import tpu as pltpu
from jax.sharding import PartitionSpec as P


RIDGE = 0.05
CORES = 2
CHIPS_DENSE = 4


def hidden_kernel(me_ref, own_names_ref, other_names_ref, gate_ref, up_ref, *refs, at, top, first):
    pieces, hidden_ref = refs[:-1], refs[-1]
    rows = hidden_ref.shape[0] // CORES
    hw = gate_ref.shape[1]
    width = 256
    mine = slice(at * top, (at + 1) * top)
    named = jnp.concatenate([own_names_ref[mine, :], other_names_ref[mine, :]], axis=0) == me_ref[0]
    named = named.astype(jnp.float32).T
    member = jnp.concatenate(
        [
            jnp.max(named[first : first + rows, c * top : (c + 1) * top], axis=1, keepdims=True)
            for c in range(CORES)
        ],
        axis=0,
    )
    x = jnp.concatenate([piece[...] for piece in pieces], axis=0)

    def step(i, carry):
        columns = pl.ds(pl.multiple_of(i * width, width), width)
        gate = jnp.dot(x, gate_ref[:, columns], preferred_element_type=jnp.float32)
        up = jnp.dot(x, up_ref[:, columns], preferred_element_type=jnp.float32)
        value = gate / (1.0 + jnp.exp(-gate)) * up
        hidden_ref[:, columns] = jnp.where(member > 0, value, 0.0).astype(jnp.bfloat16)
        return carry

    lax.fori_loop(0, hw // width, step, 0)


def hidden_of(me, pieces, names, at, top, first, gate_w, up_w):
    rows = sum(piece.shape[0] for piece in pieces)
    model, hw = gate_w.shape
    return pl.pallas_call(
        functools.partial(hidden_kernel, at=at, top=top, first=first),
        in_specs=[pl.BlockSpec(memory_space=pltpu.SMEM)] + [pl.BlockSpec(memory_space=pltpu.VMEM)] * (4 + len(pieces)),
        out_specs=pl.BlockSpec(memory_space=pltpu.VMEM),
        out_shape=jax.ShapeDtypeStruct((rows, hw), jnp.bfloat16),
        compiler_params=pltpu.CompilerParams(vmem_limit_bytes=24 << 20),
        cost_estimate=pl.CostEstimate(
            flops=2 * rows * model * 2 * hw,
            bytes_accessed=2 * (rows * model + 2 * model * hw) + 2 * rows * hw,
            transcendentals=rows * hw,
        ),
        name="hidden",
    )(me, *names, gate_w, up_w, *pieces)


def gram_of(refs):
    total = None
    for ref in refs:
        h = ref[...]
        part = lax.dot_general(h, h, (((0,), (0,)), ((), ())), preferred_element_type=jnp.float32)
        total = part if total is None else total + part
    return total


def gram_kernel(*refs):
    refs[-1][...] = gram_of(refs[:-1])


def partial_gram(hiddens):
    rows = sum(hidden.shape[0] for hidden in hiddens)
    hw = hiddens[0].shape[1]
    return pl.pallas_call(
        gram_kernel,
        in_specs=[pl.BlockSpec(memory_space=pltpu.VMEM)] * len(hiddens),
        out_specs=pl.BlockSpec(memory_space=pltpu.VMEM),
        out_shape=jax.ShapeDtypeStruct((hw, hw), jnp.float32),
        compiler_params=pltpu.CompilerParams(vmem_limit_bytes=24 << 20),
        cost_estimate=pl.CostEstimate(
            flops=2 * rows * hw * hw,
            bytes_accessed=2 * rows * hw + 4 * hw * hw,
            transcendentals=0,
        ),
        name="partial_gram",
    )(*hiddens)


def pick_kernel(chip_ref, *refs, wanted):
    sources, out_ref = refs[:-1], refs[-1]
    rows = sources[0].shape[0]
    parts = out_ref.shape[0] // rows
    kinds = len(sources) // parts
    for kind in range(kinds):
        here = functools.reduce(lambda a, b: a | b, [chip_ref[0] == c for c, k in enumerate(wanted) if k == kind])

        @pl.when(here)
        def _():
            for part in range(parts):
                out_ref[part * rows : (part + 1) * rows, :] = sources[part * kinds + kind][...]


def pick(chip, parts, wanted):
    rows, model = parts[0][0].shape
    return pl.pallas_call(
        functools.partial(pick_kernel, wanted=wanted),
        in_specs=[pl.BlockSpec(memory_space=pltpu.SMEM)]
        + [pl.BlockSpec(memory_space=pltpu.VMEM)] * sum(len(part) for part in parts),
        out_specs=pl.BlockSpec(memory_space=pltpu.VMEM),
        out_shape=jax.ShapeDtypeStruct((len(parts) * rows, model), parts[0][0].dtype),
        compiler_params=pltpu.CompilerParams(vmem_limit_bytes=8 << 20),
        cost_estimate=pl.CostEstimate(
            flops=0, bytes_accessed=4 * len(parts) * rows * model, transcendentals=0
        ),
        name="pick",
    )(chip.reshape(1), *sum(parts, []))


def between_chips(pairs):
    return [(s * CORES + c, d * CORES + c) for s, d in pairs for c in range(CORES)]


def gathered(tokens, routes, gate_w, up_w):
    me = lax.axis_index("expert").astype(jnp.int32).reshape(1)
    chip = lax.axis_index("expert") // CORES
    data_ranks = lax.axis_size("dp")
    rows, top = routes.shape
    half = rows // 2
    swap_pairs = [(e, e ^ 1) for e in range(CHIPS_DENSE * CORES)]

    def move(x, pairs):
        return lax.ppermute(x, "expert", between_chips(pairs))

    def swap(x):
        return lax.ppermute(x, "expert", swap_pairs)

    def turns(x):
        shifts = [[(r, (r + s) % data_ranks) for r in range(data_ranks)] for s in range(1, data_ranks)]
        return [x] + [lax.ppermute(x, "dp", pairs) for pairs in shifts]

    up, down = [(0, 1), (1, 2), (2, 3)], [(3, 2), (2, 1), (1, 0)]
    halves = []
    for h in range(2):
        ups, downs = [], []
        x = y = tokens[h * half : (h + 1) * half]
        for hop in range(3):
            x = move(x, up[hop:])
            y = move(y, down[hop:])
            ups.append(x)
            downs.append(y)
        halves.append((ups, downs))
    near = pick(chip, [[u[0], d[0]] for u, d in halves], (1, 0, 0, 0))
    middle = pick(chip, [[u[1], d[0], d[1]] for u, d in halves], (2, 1, 1, 0))
    last = [pick(chip, [[u[2], u[1], d[1], d[2]]], (3, 2, 1, 0)) for u, d in halves]

    names = routes.T
    by_one, by_two, by_three = (
        move(names, [(z, (z + s) % CHIPS_DENSE) for z in range(CHIPS_DENSE)]) for s in (1, 2, 3)
    )
    ends = (chip == 0) | (chip == 3)
    moved = jnp.concatenate(
        [
            jnp.where(chip == 0, by_three, by_one),
            jnp.where(ends, by_two, by_three),
            jnp.where(chip == 0, by_one, jnp.where(chip == 3, by_three, by_two)),
        ],
        axis=0,
    )
    own_names = (names, swap(names))
    moved_names = (moved, swap(moved))

    blocks = [
        (tokens, own_names, 0, 0),
        (near, moved_names, 0, 0),
        (middle, moved_names, 1, 0),
        (last[0], moved_names, 2, 0),
        (last[1], moved_names, 2, half),
    ]
    hiddens = []
    for own, who, at, first in blocks:
        pieces = (own, swap(own))
        hidden = hidden_of(me, pieces, who, at, top, first, gate_w, up_w)
        hiddens.append(turns(hidden))
    early = partial_gram(sum(hiddens[:-1], []))
    return early, hiddens[-1]


def packed_grams(tokens, routes, gate_w, up_w, capacity):
    owners = lax.axis_size("expert")
    experts = owners
    model_width = tokens.shape[1]
    tok_rows, top_count = routes.shape
    assigned = routes.reshape(-1)
    onehot = (assigned[:, None] == jnp.arange(experts, dtype=jnp.int32)[None, :]).astype(jnp.int32)
    position = jnp.sum(jnp.cumsum(onehot, axis=0) * onehot, axis=1) - 1
    target = assigned * capacity + position
    anchor = jnp.arange(tok_rows * top_count, dtype=jnp.int32) // top_count
    source_row = jnp.zeros((experts * capacity,), jnp.int32).at[target].set(anchor)
    filled = jnp.zeros((experts * capacity,), jnp.int32).at[target].set(1)
    outbox = jnp.where(filled[:, None] > 0, tokens[source_row], jnp.zeros((), tokens.dtype))
    outbox = outbox.reshape(experts, capacity, model_width)
    arrived = lax.all_to_all(outbox, "expert", split_axis=0, concat_axis=0, tiled=True)
    flattened = arrived.reshape(-1, model_width)
    gate_proj = jnp.dot(flattened, gate_w, preferred_element_type=jnp.float32)
    up_proj = jnp.dot(flattened, up_w, preferred_element_type=jnp.float32)
    hidden = (jax.nn.silu(gate_proj) * up_proj).astype(jnp.bfloat16)
    return lax.dot_general(hidden, hidden, (((0,), (0,)), ((), ())), preferred_element_type=jnp.float32)


def body(tokens, routes, w_gate, w_up):
    owners = lax.axis_size("expert")
    data_ranks = lax.axis_size("dp")
    experts = w_gate.shape[0] * owners
    tok_rows, top_count = routes.shape
    capacity = min(tok_rows, 2 * tok_rows * top_count // experts)
    gate_w, up_w = w_gate[0], w_up[0]
    if tok_rows * owners <= experts * capacity and owners == CHIPS_DENSE * CORES:
        early, late = gathered(tokens, routes, gate_w, up_w)
    else:
        gram = packed_grams(tokens, routes, gate_w, up_w, capacity)
        early, late = gram, []
        for s in range(1, data_ranks):
            early = early + lax.ppermute(gram, "dp", [(r, (r + s) % data_ranks) for r in range(data_ranks)])
    rows_mean = data_ranks * tok_rows * top_count
    return factor_rows(early, late, rows_mean, data_ranks)[None]


def over_lanes(column, width):
    return jnp.concatenate([column] * (width // column.shape[1]), axis=1)


def factor_panel(x, columns, sublane):
    rows, width = x.shape
    factor = jnp.zeros_like(x)
    for k in range(rows):
        scale = lax.rsqrt(jnp.broadcast_to(columns[k][k : k + 1, :], columns[k].shape))
        lower = columns[k] * scale
        upper = jnp.broadcast_to(x[k : k + 1, :], x.shape) * over_lanes(scale, width)
        factor = jnp.where(sublane == k, upper, factor)
        for j in range(k + 1, rows):
            columns[j] = columns[j] - lower * jnp.broadcast_to(lower[j : j + 1, :], lower.shape)
        if k + 1 < rows:
            x = x - over_lanes(lower, width) * upper
    return factor


def outer_sum(a, b):
    return lax.dot_general(
        a, b, (((0,), (0,)), ((), ())), precision=lax.Precision.HIGHEST, preferred_element_type=jnp.float32
    )


def factor_kernel(rank_ref, early_ref, *refs, rows_mean):
    late_refs, (my_rows_ref, out_ref, rest_ref) = refs[:-3], refs[-3:]
    size = early_ref.shape[0]
    block, panel = 128, 8
    row = lax.broadcasted_iota(jnp.int32, (size, size), 0)
    col = lax.broadcasted_iota(jnp.int32, (size, size), 1)
    gram = early_ref[...]
    if late_refs:
        gram = gram + gram_of(late_refs)
    rest_ref[...] = gram / rows_mean + jnp.where(row == col, RIDGE, 0.0)
    for base in range(0, size, block):
        width = size - base
        end = base + block
        if base:
            out_ref[base:end, :base] = jnp.zeros((block, base), jnp.float32)
        sublane = lax.broadcasted_iota(jnp.int32, (panel, width), 0)
        lane = lax.broadcasted_iota(jnp.int32, (panel, width), 1)

        def step(p, carry):
            first = panel * p
            rows = pl.ds(pl.multiple_of(base + first, panel), panel)
            x = rest_ref[rows, base:]
            corner = x[:, :block]
            columns = [
                jnp.take_along_axis(
                    corner, jnp.full(corner.shape, first + j, jnp.int32), axis=1, mode="promise_in_bounds"
                )
                for j in range(panel)
            ]
            factor = factor_panel(x, columns, sublane)
            out_ref[rows, base:] = jnp.where(lane >= sublane + first, factor, 0.0)
            below = jnp.where(lane[:, :block] >= first + panel, factor[:, :block], 0.0)
            rest_ref[base:end, base:] -= outer_sum(below, factor)
            return carry

        lax.fori_loop(0, block // panel, step, 0)
        if end < size:
            done = out_ref[base:end, end:]
            rest_ref[end:, end:] -= outer_sum(done, done)
    count = my_rows_ref.shape[0]
    my_rows_ref[...] = out_ref[pl.ds(pl.multiple_of(rank_ref[0] * count, count), count), :]


def factor_rows(early, late, rows_mean, data_ranks):
    size = early.shape[0]
    rank = lax.axis_index("dp").astype(jnp.int32).reshape(1)
    return pl.pallas_call(
        functools.partial(factor_kernel, rows_mean=rows_mean),
        in_specs=[pl.BlockSpec(memory_space=pltpu.SMEM)] + [pl.BlockSpec(memory_space=pltpu.VMEM)] * (1 + len(late)),
        out_specs=pl.BlockSpec(memory_space=pltpu.VMEM),
        out_shape=jax.ShapeDtypeStruct((size // data_ranks, size), jnp.float32),
        scratch_shapes=[pltpu.VMEM((size, size), jnp.float32)] * 2,
        compiler_params=pltpu.CompilerParams(vmem_limit_bytes=24 << 20),
        name="factor",
    )(rank, early, *late)


def solution(mesh):
    in_specs = (
        P(("groups", "dp", "expert"), None),
        P(("groups", "dp", "expert"), None),
        P(("groups", "expert"), None, None),
        P(("groups", "expert"), None, None),
    )
    out_specs = P(("groups", "expert"), "dp", None)
    return jax.shard_map(body, mesh=mesh, in_specs=in_specs, out_specs=out_specs, check_vma=False)
```

```python
import functools

import jax
import jax.numpy as jnp
from jax import lax
from jax.experimental import pallas as pl
from jax.experimental.pallas import tpu as pltpu
from jax.sharding import PartitionSpec as P


RIDGE = 0.05
CORES = 2
CHIPS_DENSE = 4


def hidden_kernel(me_ref, own_ref, other_ref, own_names_ref, other_names_ref, gate_ref, up_ref, hidden_ref, *, at, top):
    hw = gate_ref.shape[1]
    width = 256
    mine = slice(at * top, (at + 1) * top)
    named = jnp.concatenate([own_names_ref[mine, :], other_names_ref[mine, :]], axis=0) == me_ref[0]
    named = named.astype(jnp.float32).T
    member = jnp.concatenate(
        [jnp.max(named[:, c * top : (c + 1) * top], axis=1, keepdims=True) for c in range(CORES)], axis=0
    )
    x = jnp.concatenate([own_ref[...], other_ref[...]], axis=0)

    def step(i, carry):
        columns = pl.ds(pl.multiple_of(i * width, width), width)
        gate = jnp.dot(x, gate_ref[:, columns], preferred_element_type=jnp.float32)
        up = jnp.dot(x, up_ref[:, columns], preferred_element_type=jnp.float32)
        value = gate / (1.0 + jnp.exp(-gate)) * up
        hidden_ref[:, columns] = jnp.where(member > 0, value, 0.0).astype(jnp.bfloat16)
        return carry

    lax.fori_loop(0, hw // width, step, 0)


def hidden_of(me, own, other, own_names, other_names, at, top, gate_w, up_w):
    rows, model = own.shape
    hw = gate_w.shape[1]
    return pl.pallas_call(
        functools.partial(hidden_kernel, at=at, top=top),
        in_specs=[pl.BlockSpec(memory_space=pltpu.SMEM)] + [pl.BlockSpec(memory_space=pltpu.VMEM)] * 6,
        out_specs=pl.BlockSpec(memory_space=pltpu.VMEM),
        out_shape=jax.ShapeDtypeStruct((CORES * rows, hw), jnp.bfloat16),
        compiler_params=pltpu.CompilerParams(vmem_limit_bytes=24 << 20),
        cost_estimate=pl.CostEstimate(
            flops=2 * CORES * rows * model * 2 * hw,
            bytes_accessed=2 * (CORES * rows * model + 2 * model * hw) + 2 * CORES * rows * hw,
            transcendentals=CORES * rows * hw,
        ),
        name="hidden",
    )(me, own, other, own_names, other_names, gate_w, up_w)


def gram_of(refs):
    total = None
    for ref in refs:
        h = ref[...]
        part = lax.dot_general(h, h, (((0,), (0,)), ((), ())), preferred_element_type=jnp.float32)
        total = part if total is None else total + part
    return total


def gram_kernel(*refs):
    refs[-1][...] = gram_of(refs[:-1])


def partial_gram(hiddens):
    rows, hw = hiddens[0].shape
    return pl.pallas_call(
        gram_kernel,
        in_specs=[pl.BlockSpec(memory_space=pltpu.VMEM)] * len(hiddens),
        out_specs=pl.BlockSpec(memory_space=pltpu.VMEM),
        out_shape=jax.ShapeDtypeStruct((hw, hw), jnp.float32),
        compiler_params=pltpu.CompilerParams(vmem_limit_bytes=24 << 20),
        cost_estimate=pl.CostEstimate(
            flops=2 * len(hiddens) * rows * hw * hw,
            bytes_accessed=2 * len(hiddens) * rows * hw + 4 * hw * hw,
            transcendentals=0,
        ),
        name="partial_gram",
    )(*hiddens)


def between_chips(pairs):
    return [(s * CORES + c, d * CORES + c) for s, d in pairs for c in range(CORES)]


def gathered(tokens, routes, gate_w, up_w):
    me = lax.axis_index("expert").astype(jnp.int32).reshape(1)
    data_ranks = lax.axis_size("dp")
    top = routes.shape[1]
    move = lambda x, pairs: lax.ppermute(x, "expert", between_chips(pairs))
    swap = lambda x: lax.ppermute(x, "expert", [(e, e ^ 1) for e in range(CHIPS_DENSE * CORES)])
    turn = lambda x, s: lax.ppermute(x, "dp", [(r, (r + s) % data_ranks) for r in range(data_ranks)])
    ring = lambda s: [(z, (z + s) % CHIPS_DENSE) for z in range(CHIPS_DENSE)]

    names = routes.T
    below = move(tokens, ring(1))
    above = move(tokens, ring(-1))
    on_up = move(below, [(1, 2), (2, 3)])
    on_down = move(above, [(2, 1), (1, 0)])
    moved = []
    for pairs in [ring(1), ring(-1), ring(2)]:
        moved.append(move(names, pairs))
    moved = jnp.concatenate(moved, axis=0)
    other_names = swap(names)
    other_moved = swap(moved)

    hiddens = []
    for slot, own in enumerate([tokens, below, above, on_up + on_down]):
        other = swap(own)
        if slot == 0:
            hidden = hidden_of(me, own, other, names, other_names, 0, top, gate_w, up_w)
        else:
            hidden = hidden_of(me, own, other, moved, other_moved, slot - 1, top, gate_w, up_w)
        hiddens.append([hidden] + [turn(hidden, s) for s in range(1, data_ranks)])
    early = partial_gram(sum(hiddens[:-1], []))
    return early, hiddens[-1]


def packed_grams(tokens, routes, gate_w, up_w, capacity):
    owners = lax.axis_size("expert")
    experts = owners
    model_width = tokens.shape[1]
    tok_rows, top_count = routes.shape
    assigned = routes.reshape(-1)
    onehot = (assigned[:, None] == jnp.arange(experts, dtype=jnp.int32)[None, :]).astype(jnp.int32)
    position = jnp.sum(jnp.cumsum(onehot, axis=0) * onehot, axis=1) - 1
    target = assigned * capacity + position
    anchor = jnp.arange(tok_rows * top_count, dtype=jnp.int32) // top_count
    source_row = jnp.zeros((experts * capacity,), jnp.int32).at[target].set(anchor)
    filled = jnp.zeros((experts * capacity,), jnp.int32).at[target].set(1)
    outbox = jnp.where(filled[:, None] > 0, tokens[source_row], jnp.zeros((), tokens.dtype))
    outbox = outbox.reshape(experts, capacity, model_width)
    arrived = lax.all_to_all(outbox, "expert", split_axis=0, concat_axis=0, tiled=True)
    flattened = arrived.reshape(-1, model_width)
    gate_proj = jnp.dot(flattened, gate_w, preferred_element_type=jnp.float32)
    up_proj = jnp.dot(flattened, up_w, preferred_element_type=jnp.float32)
    hidden = (jax.nn.silu(gate_proj) * up_proj).astype(jnp.bfloat16)
    return lax.dot_general(hidden, hidden, (((0,), (0,)), ((), ())), preferred_element_type=jnp.float32)


def body(tokens, routes, w_gate, w_up):
    owners = lax.axis_size("expert")
    data_ranks = lax.axis_size("dp")
    experts = w_gate.shape[0] * owners
    tok_rows, top_count = routes.shape
    capacity = min(tok_rows, 2 * tok_rows * top_count // experts)
    gate_w, up_w = w_gate[0], w_up[0]
    if tok_rows * owners <= experts * capacity and owners == CHIPS_DENSE * CORES:
        early, late = gathered(tokens, routes, gate_w, up_w)
    else:
        gram = packed_grams(tokens, routes, gate_w, up_w, capacity)
        early, late = gram, []
        for s in range(1, data_ranks):
            early = early + lax.ppermute(gram, "dp", [(r, (r + s) % data_ranks) for r in range(data_ranks)])
    rows_mean = data_ranks * tok_rows * top_count
    return factor_rows(early, late, rows_mean, data_ranks)[None]


def over_lanes(column, width):
    return jnp.concatenate([column] * (width // column.shape[1]), axis=1)


def factor_panel(x, columns, sublane):
    rows, width = x.shape
    factor = jnp.zeros_like(x)
    for k in range(rows):
        scale = lax.rsqrt(jnp.broadcast_to(columns[k][k : k + 1, :], columns[k].shape))
        lower = columns[k] * scale
        upper = jnp.broadcast_to(x[k : k + 1, :], x.shape) * over_lanes(scale, width)
        factor = jnp.where(sublane == k, upper, factor)
        for j in range(k + 1, rows):
            columns[j] = columns[j] - lower * jnp.broadcast_to(lower[j : j + 1, :], lower.shape)
        if k + 1 < rows:
            x = x - over_lanes(lower, width) * upper
    return factor


def outer_sum(a, b):
    return lax.dot_general(
        a, b, (((0,), (0,)), ((), ())), precision=lax.Precision.HIGHEST, preferred_element_type=jnp.float32
    )


def factor_kernel(rank_ref, early_ref, *refs, rows_mean):
    late_refs, (my_rows_ref, out_ref, rest_ref) = refs[:-3], refs[-3:]
    size = early_ref.shape[0]
    block, panel = 128, 8
    row = lax.broadcasted_iota(jnp.int32, (size, size), 0)
    col = lax.broadcasted_iota(jnp.int32, (size, size), 1)
    gram = early_ref[...]
    if late_refs:
        gram = gram + gram_of(late_refs)
    rest_ref[...] = gram / rows_mean + jnp.where(row == col, RIDGE, 0.0)
    for base in range(0, size, block):
        width = size - base
        end = base + block
        if base:
            out_ref[base:end, :base] = jnp.zeros((block, base), jnp.float32)
        sublane = lax.broadcasted_iota(jnp.int32, (panel, width), 0)
        lane = lax.broadcasted_iota(jnp.int32, (panel, width), 1)

        def step(p, carry):
            first = panel * p
            rows = pl.ds(pl.multiple_of(base + first, panel), panel)
            x = rest_ref[rows, base:]
            corner = x[:, :block]
            columns = [
                jnp.take_along_axis(
                    corner, jnp.full(corner.shape, first + j, jnp.int32), axis=1, mode="promise_in_bounds"
                )
                for j in range(panel)
            ]
            factor = factor_panel(x, columns, sublane)
            out_ref[rows, base:] = jnp.where(lane >= sublane + first, factor, 0.0)
            below = jnp.where(lane[:, :block] >= first + panel, factor[:, :block], 0.0)
            rest_ref[base:end, base:] -= outer_sum(below, factor)
            return carry

        lax.fori_loop(0, block // panel, step, 0)
        if end < size:
            done = out_ref[base:end, end:]
            rest_ref[end:, end:] -= outer_sum(done, done)
    count = my_rows_ref.shape[0]
    my_rows_ref[...] = out_ref[pl.ds(pl.multiple_of(rank_ref[0] * count, count), count), :]


def factor_rows(early, late, rows_mean, data_ranks):
    size = early.shape[0]
    rank = lax.axis_index("dp").astype(jnp.int32).reshape(1)
    return pl.pallas_call(
        functools.partial(factor_kernel, rows_mean=rows_mean),
        in_specs=[pl.BlockSpec(memory_space=pltpu.SMEM)] + [pl.BlockSpec(memory_space=pltpu.VMEM)] * (1 + len(late)),
        out_specs=pl.BlockSpec(memory_space=pltpu.VMEM),
        out_shape=jax.ShapeDtypeStruct((size // data_ranks, size), jnp.float32),
        scratch_shapes=[pltpu.VMEM((size, size), jnp.float32)] * 2,
        compiler_params=pltpu.CompilerParams(vmem_limit_bytes=24 << 20),
        name="factor",
    )(rank, early, *late)


def solution(mesh):
    in_specs = (
        P(("groups", "dp", "expert"), None),
        P(("groups", "dp", "expert"), None),
        P(("groups", "expert"), None, None),
        P(("groups", "expert"), None, None),
    )
    out_specs = P(("groups", "expert"), "dp", None)
    return jax.shard_map(body, mesh=mesh, in_specs=in_specs, out_specs=out_specs, check_vma=False)
```

```python
import functools

import jax
import jax.numpy as jnp
from jax import lax
from jax.experimental import pallas as pl
from jax.experimental.pallas import tpu as pltpu
from jax.sharding import PartitionSpec as P


RIDGE = 0.05
CORES = 2
CHIPS_DENSE = 4


def hidden_kernel(me_ref, own_ref, other_ref, own_names_ref, other_names_ref, gate_ref, up_ref, hidden_ref, *, at, top):
    hw = gate_ref.shape[1]
    width = 256
    mine = slice(at * top, (at + 1) * top)
    named = jnp.concatenate([own_names_ref[mine, :], other_names_ref[mine, :]], axis=0) == me_ref[0]
    named = named.astype(jnp.float32).T
    member = jnp.concatenate(
        [jnp.max(named[:, c * top : (c + 1) * top], axis=1, keepdims=True) for c in range(CORES)], axis=0
    )
    x = jnp.concatenate([own_ref[...], other_ref[...]], axis=0)

    def step(i, carry):
        columns = pl.ds(pl.multiple_of(i * width, width), width)
        gate = jnp.dot(x, gate_ref[:, columns], preferred_element_type=jnp.float32)
        up = jnp.dot(x, up_ref[:, columns], preferred_element_type=jnp.float32)
        value = gate / (1.0 + jnp.exp(-gate)) * up
        hidden_ref[:, columns] = jnp.where(member > 0, value, 0.0).astype(jnp.bfloat16)
        return carry

    lax.fori_loop(0, hw // width, step, 0)


def hidden_of(me, own, other, own_names, other_names, at, top, gate_w, up_w):
    rows, model = own.shape
    hw = gate_w.shape[1]
    return pl.pallas_call(
        functools.partial(hidden_kernel, at=at, top=top),
        in_specs=[pl.BlockSpec(memory_space=pltpu.SMEM)] + [pl.BlockSpec(memory_space=pltpu.VMEM)] * 6,
        out_specs=pl.BlockSpec(memory_space=pltpu.VMEM),
        out_shape=jax.ShapeDtypeStruct((CORES * rows, hw), jnp.bfloat16),
        compiler_params=pltpu.CompilerParams(vmem_limit_bytes=24 << 20),
        cost_estimate=pl.CostEstimate(
            flops=2 * CORES * rows * model * 2 * hw,
            bytes_accessed=2 * (CORES * rows * model + 2 * model * hw) + 2 * CORES * rows * hw,
            transcendentals=CORES * rows * hw,
        ),
        name="hidden",
    )(me, own, other, own_names, other_names, gate_w, up_w)


def gram_of(refs):
    total = None
    for ref in refs:
        h = ref[...]
        part = lax.dot_general(h, h, (((0,), (0,)), ((), ())), preferred_element_type=jnp.float32)
        total = part if total is None else total + part
    return total


def gram_kernel(*refs):
    refs[-1][...] = gram_of(refs[:-1])


def partial_gram(hiddens):
    rows, hw = hiddens[0].shape
    return pl.pallas_call(
        gram_kernel,
        in_specs=[pl.BlockSpec(memory_space=pltpu.VMEM)] * len(hiddens),
        out_specs=pl.BlockSpec(memory_space=pltpu.VMEM),
        out_shape=jax.ShapeDtypeStruct((hw, hw), jnp.float32),
        compiler_params=pltpu.CompilerParams(vmem_limit_bytes=24 << 20),
        cost_estimate=pl.CostEstimate(
            flops=2 * len(hiddens) * rows * hw * hw,
            bytes_accessed=2 * len(hiddens) * rows * hw + 4 * hw * hw,
            transcendentals=0,
        ),
        name="partial_gram",
    )(*hiddens)


def between_chips(pairs):
    return [(s * CORES + c, d * CORES + c) for s, d in pairs for c in range(CORES)]


def gathered(tokens, routes, gate_w, up_w):
    me = lax.axis_index("expert").astype(jnp.int32).reshape(1)
    data_ranks = lax.axis_size("dp")
    top = routes.shape[1]
    move = lambda x, pairs: lax.ppermute(x, "expert", between_chips(pairs))
    swap = lambda x: lax.ppermute(x, "expert", [(e, e ^ 1) for e in range(CHIPS_DENSE * CORES)])
    turn = lambda x, s: lax.ppermute(x, "dp", [(r, (r + s) % data_ranks) for r in range(data_ranks)])
    ring = lambda s: [(z, (z + s) % CHIPS_DENSE) for z in range(CHIPS_DENSE)]

    names = routes.T
    below = move(tokens, ring(1))
    above = move(tokens, ring(-1))
    on_up = move(below, [(1, 2), (2, 3)])
    on_down = move(above, [(2, 1), (1, 0)])
    moved = []
    for pairs in [ring(1), ring(-1), ring(2)]:
        moved.append(move(names, pairs))
    moved = jnp.concatenate(moved, axis=0)
    other_names = swap(names)
    other_moved = swap(moved)

    hiddens = []
    for slot, own in enumerate([tokens, below, above, on_up + on_down]):
        other = swap(own)
        if slot == 0:
            hidden = hidden_of(me, own, other, names, other_names, 0, top, gate_w, up_w)
        else:
            hidden = hidden_of(me, own, other, moved, other_moved, slot - 1, top, gate_w, up_w)
        hiddens.append([hidden] + [turn(hidden, s) for s in range(1, data_ranks)])
    early = partial_gram(sum(hiddens[:-1], []))
    return early, hiddens[-1]


def packed_grams(tokens, routes, gate_w, up_w, capacity):
    owners = lax.axis_size("expert")
    experts = owners
    model_width = tokens.shape[1]
    tok_rows, top_count = routes.shape
    assigned = routes.reshape(-1)
    onehot = (assigned[:, None] == jnp.arange(experts, dtype=jnp.int32)[None, :]).astype(jnp.int32)
    position = jnp.sum(jnp.cumsum(onehot, axis=0) * onehot, axis=1) - 1
    target = assigned * capacity + position
    anchor = jnp.arange(tok_rows * top_count, dtype=jnp.int32) // top_count
    source_row = jnp.zeros((experts * capacity,), jnp.int32).at[target].set(anchor)
    filled = jnp.zeros((experts * capacity,), jnp.int32).at[target].set(1)
    outbox = jnp.where(filled[:, None] > 0, tokens[source_row], jnp.zeros((), tokens.dtype))
    outbox = outbox.reshape(experts, capacity, model_width)
    arrived = lax.all_to_all(outbox, "expert", split_axis=0, concat_axis=0, tiled=True)
    flattened = arrived.reshape(-1, model_width)
    gate_proj = jnp.dot(flattened, gate_w, preferred_element_type=jnp.float32)
    up_proj = jnp.dot(flattened, up_w, preferred_element_type=jnp.float32)
    hidden = (jax.nn.silu(gate_proj) * up_proj).astype(jnp.bfloat16)
    return lax.dot_general(hidden, hidden, (((0,), (0,)), ((), ())), preferred_element_type=jnp.float32)


def body(tokens, routes, w_gate, w_up):
    owners = lax.axis_size("expert")
    data_ranks = lax.axis_size("dp")
    experts = w_gate.shape[0] * owners
    tok_rows, top_count = routes.shape
    capacity = min(tok_rows, 2 * tok_rows * top_count // experts)
    gate_w, up_w = w_gate[0], w_up[0]
    if tok_rows * owners <= experts * capacity and owners == CHIPS_DENSE * CORES:
        early, late = gathered(tokens, routes, gate_w, up_w)
    else:
        gram = packed_grams(tokens, routes, gate_w, up_w, capacity)
        early, late = gram, []
        for s in range(1, data_ranks):
            early = early + lax.ppermute(gram, "dp", [(r, (r + s) % data_ranks) for r in range(data_ranks)])
    rows_mean = data_ranks * tok_rows * top_count
    return factor_rows(early, late, rows_mean, data_ranks)[None]


def over_lanes(column, width):
    return jnp.concatenate([column] * (width // column.shape[1]), axis=1)


def row_of(x, k):
    return jnp.broadcast_to(x[k : k + 1, :], x.shape)


def lane_of(x, at):
    return jnp.take_along_axis(x, jnp.full(x.shape, at, jnp.int32), axis=1, mode="promise_in_bounds")


PRODUCTS = ((0, 0), (0, 1), (1, 0), (0, 2), (2, 0), (1, 1))


def three_parts(x):
    high = x.astype(jnp.bfloat16).astype(jnp.float32)
    rest = x - high
    middle = rest.astype(jnp.bfloat16).astype(jnp.float32)
    return high, middle, rest - middle


def outer_of_few(a, b):
    left, right = three_parts(a), three_parts(b)
    left = jnp.concatenate([left[i] for i, _ in PRODUCTS], axis=0)
    right = jnp.concatenate([right[j] for _, j in PRODUCTS], axis=0).astype(jnp.bfloat16)
    return jnp.dot(left.T.astype(jnp.bfloat16), right, preferred_element_type=jnp.float32)


def outer_of_many(a, b):
    left, right = three_parts(a.T), three_parts(b)
    left = jnp.concatenate([left[i].astype(jnp.bfloat16) for i, _ in PRODUCTS], axis=1)
    right = jnp.concatenate([right[j].astype(jnp.bfloat16) for _, j in PRODUCTS], axis=0)
    return jnp.dot(left, right, preferred_element_type=jnp.float32)


def factor_panel(rows, columns, sublane):
    group, width = rows[0].shape
    count = len(rows)
    done = []
    for s in range(count):
        factor = jnp.zeros_like(rows[s])
        for k in range(group):
            pivot = columns[s][s][k]
            scale = lax.rsqrt(row_of(pivot, k))
            lower = {t: columns[t][s][k] * scale for t in range(s, count)}
            upper = row_of(rows[s], k) * over_lanes(scale, width)
            factor = jnp.where(sublane == k, upper, factor)
            for u in range(s, count):
                for j in range(k + 1 if u == s else 0, group):
                    entry = row_of(lower[u], j)
                    for t in range(u, count):
                        columns[t][u][j] = columns[t][u][j] - lower[t] * entry
            for t in range(s if k + 1 < group else s + 1, count):
                rows[t] = rows[t] - over_lanes(lower[t], width) * upper
        done.append(factor)
    return done


def factor_kernel(rank_ref, early_ref, *refs, rows_mean):
    late_refs, (my_rows_ref, out_ref, rest_ref) = refs[:-3], refs[-3:]
    size = early_ref.shape[0]
    block, group, groups = 128, 8, 4
    panel = group * groups
    row = lax.broadcasted_iota(jnp.int32, (size, size), 0)
    col = lax.broadcasted_iota(jnp.int32, (size, size), 1)
    gram = early_ref[...]
    if late_refs:
        gram = gram + gram_of(late_refs)
    rest_ref[...] = gram / rows_mean + jnp.where(row == col, RIDGE, 0.0)
    for base in range(0, size, block):
        width = size - base
        end = base + block
        if base:
            out_ref[base:end, :base] = jnp.zeros((block, base), jnp.float32)
        sublane = lax.broadcasted_iota(jnp.int32, (group, width), 0)
        lane = lax.broadcasted_iota(jnp.int32, (group, width), 1)
        panel_lane = lax.broadcasted_iota(jnp.int32, (panel, block), 1)

        def step(p, carry):
            first = panel * p
            at = [pl.ds(pl.multiple_of(base + first + group * t, group), group) for t in range(groups)]
            rows = [rest_ref[at[t], base:] for t in range(groups)]
            columns = [
                [[lane_of(rows[t][:, :block], first + group * u + j) for j in range(group)] for u in range(t + 1)]
                for t in range(groups)
            ]
            done = factor_panel(rows, columns, sublane)
            for t in range(groups):
                out_ref[at[t], base:] = jnp.where(lane >= sublane + first + group * t, done[t], 0.0)
            done = jnp.concatenate(done, axis=0)
            below = jnp.where(panel_lane >= first + panel, done[:, :block], 0.0)
            rest_ref[base:end, base:] -= outer_of_few(below, done)
            return carry

        lax.fori_loop(0, block // panel, step, 0)
        for to in range(end, size, block):
            right = out_ref[base:end, to:]
            rest_ref[to : to + block, to:] -= outer_of_many(right[:, :block], right)
    count = my_rows_ref.shape[0]
    my_rows_ref[...] = out_ref[pl.ds(pl.multiple_of(rank_ref[0] * count, count), count), :]


def factor_rows(early, late, rows_mean, data_ranks):
    size = early.shape[0]
    rank = lax.axis_index("dp").astype(jnp.int32).reshape(1)
    return pl.pallas_call(
        functools.partial(factor_kernel, rows_mean=rows_mean),
        in_specs=[pl.BlockSpec(memory_space=pltpu.SMEM)] + [pl.BlockSpec(memory_space=pltpu.VMEM)] * (1 + len(late)),
        out_specs=pl.BlockSpec(memory_space=pltpu.VMEM),
        out_shape=jax.ShapeDtypeStruct((size // data_ranks, size), jnp.float32),
        scratch_shapes=[pltpu.VMEM((size, size), jnp.float32)] * 2,
        compiler_params=pltpu.CompilerParams(vmem_limit_bytes=24 << 20),
        name="factor",
    )(rank, early, *late)


def solution(mesh):
    in_specs = (
        P(("groups", "dp", "expert"), None),
        P(("groups", "dp", "expert"), None),
        P(("groups", "expert"), None, None),
        P(("groups", "expert"), None, None),
    )
    out_specs = P(("groups", "expert"), "dp", None)
    return jax.shard_map(body, mesh=mesh, in_specs=in_specs, out_specs=out_specs, check_vma=False)
```

```python
import functools

import jax
import jax.numpy as jnp
from jax import lax
from jax.experimental import pallas as pl
from jax.experimental.pallas import tpu as pltpu
from jax.sharding import PartitionSpec as P


RIDGE = 0.05
CORES = 2
CHIPS_DENSE = 4


def hidden_kernel(me_ref, gate_ref, up_ref, *refs, at, top):
    hidden_ref = refs[-1]
    count = len(refs) // 2
    pieces, names = refs[:count], refs[count:-1]
    hw = gate_ref.shape[1]
    width = 256
    member = []
    for name in names:
        hit = (name[at * top : (at + 1) * top, :] == me_ref[0]).astype(jnp.float32)
        member.append(jnp.max(hit.T, axis=1, keepdims=True))
    member = jnp.concatenate(member, axis=0)
    x = jnp.concatenate([piece[...] for piece in pieces], axis=0)

    def step(i, carry):
        columns = pl.ds(pl.multiple_of(i * width, width), width)
        gate = jnp.dot(x, gate_ref[:, columns], preferred_element_type=jnp.float32)
        up = jnp.dot(x, up_ref[:, columns], preferred_element_type=jnp.float32)
        value = gate / (1.0 + jnp.exp(-gate)) * up
        hidden_ref[:, columns] = jnp.where(member > 0, value, 0.0).astype(jnp.bfloat16)
        return carry

    lax.fori_loop(0, hw // width, step, 0)


def hidden_of(me, pieces, names, at, top, gate_w, up_w):
    rows = sum(piece.shape[0] for piece in pieces)
    model, hw = gate_w.shape
    return pl.pallas_call(
        functools.partial(hidden_kernel, at=at, top=top),
        in_specs=[pl.BlockSpec(memory_space=pltpu.SMEM)]
        + [pl.BlockSpec(memory_space=pltpu.VMEM)] * (2 + 2 * len(pieces)),
        out_specs=pl.BlockSpec(memory_space=pltpu.VMEM),
        out_shape=jax.ShapeDtypeStruct((rows, hw), jnp.bfloat16),
        compiler_params=pltpu.CompilerParams(vmem_limit_bytes=24 << 20),
        cost_estimate=pl.CostEstimate(
            flops=2 * rows * model * 2 * hw,
            bytes_accessed=2 * (rows * model + 2 * model * hw) + 2 * rows * hw,
            transcendentals=rows * hw,
        ),
        name="hidden",
    )(me, gate_w, up_w, *pieces, *names)


def gram_of(refs):
    total = None
    for ref in refs:
        h = ref[...]
        part = lax.dot_general(h, h, (((0,), (0,)), ((), ())), preferred_element_type=jnp.float32)
        total = part if total is None else total + part
    return total


def gram_kernel(*refs):
    refs[-1][...] = gram_of(refs[:-1])


def partial_gram(hiddens):
    rows = sum(hidden.shape[0] for hidden in hiddens)
    hw = hiddens[0].shape[1]
    return pl.pallas_call(
        gram_kernel,
        in_specs=[pl.BlockSpec(memory_space=pltpu.VMEM)] * len(hiddens),
        out_specs=pl.BlockSpec(memory_space=pltpu.VMEM),
        out_shape=jax.ShapeDtypeStruct((hw, hw), jnp.float32),
        compiler_params=pltpu.CompilerParams(vmem_limit_bytes=24 << 20),
        cost_estimate=pl.CostEstimate(
            flops=2 * rows * hw * hw,
            bytes_accessed=2 * rows * hw + 4 * hw * hw,
            transcendentals=0,
        ),
        name="partial_gram",
    )(*hiddens)


def between_chips(pairs):
    return [(s * CORES + c, d * CORES + c) for s, d in pairs for c in range(CORES)]


def gathered(tokens, routes, gate_w, up_w):
    me = lax.axis_index("expert").astype(jnp.int32).reshape(1)
    data_ranks = lax.axis_size("dp")
    top = routes.shape[1]
    move = lambda x, pairs: lax.ppermute(x, "expert", between_chips(pairs))
    swap = lambda x: lax.ppermute(x, "expert", [(e, e ^ 1) for e in range(CHIPS_DENSE * CORES)])
    turn = lambda x, s: lax.ppermute(x, "dp", [(r, (r + s) % data_ranks) for r in range(data_ranks)])
    ring = lambda s: [(z, (z + s) % CHIPS_DENSE) for z in range(CHIPS_DENSE)]

    names = routes.T
    above = move(tokens, ring(-1))
    below = move(tokens, ring(1))
    on_down = move(above, [(2, 1), (1, 0)])
    on_up = move(below, [(1, 2), (2, 3)])
    moved = []
    for pairs in [ring(-1), ring(1), ring(2)]:
        moved.append(move(names, pairs))
    moved = jnp.concatenate(moved, axis=0)
    other_names = swap(names)
    other_moved = swap(moved)

    hiddens = []
    for slot, own in enumerate([tokens, above, below]):
        other = swap(own)
        who, at = ((names, other_names), 0) if slot == 0 else ((moved, other_moved), slot - 1)
        hidden = hidden_of(me, (own, other), who, at, top, gate_w, up_w)
        hiddens.append([hidden] + [turn(hidden, s) for s in range(1, data_ranks)])
    early = partial_gram(sum(hiddens, []))

    last = on_up + on_down
    other = swap(last)
    late = []
    for piece, who in ((last, moved), (other, other_moved)):
        hidden = hidden_of(me, (piece,), (who,), 2, top, gate_w, up_w)
        late += [hidden] + [turn(hidden, s) for s in range(1, data_ranks)]
    return early, late


def packed_grams(tokens, routes, gate_w, up_w, capacity):
    owners = lax.axis_size("expert")
    experts = owners
    model_width = tokens.shape[1]
    tok_rows, top_count = routes.shape
    assigned = routes.reshape(-1)
    onehot = (assigned[:, None] == jnp.arange(experts, dtype=jnp.int32)[None, :]).astype(jnp.int32)
    position = jnp.sum(jnp.cumsum(onehot, axis=0) * onehot, axis=1) - 1
    target = assigned * capacity + position
    anchor = jnp.arange(tok_rows * top_count, dtype=jnp.int32) // top_count
    source_row = jnp.zeros((experts * capacity,), jnp.int32).at[target].set(anchor)
    filled = jnp.zeros((experts * capacity,), jnp.int32).at[target].set(1)
    outbox = jnp.where(filled[:, None] > 0, tokens[source_row], jnp.zeros((), tokens.dtype))
    outbox = outbox.reshape(experts, capacity, model_width)
    arrived = lax.all_to_all(outbox, "expert", split_axis=0, concat_axis=0, tiled=True)
    flattened = arrived.reshape(-1, model_width)
    gate_proj = jnp.dot(flattened, gate_w, preferred_element_type=jnp.float32)
    up_proj = jnp.dot(flattened, up_w, preferred_element_type=jnp.float32)
    hidden = (jax.nn.silu(gate_proj) * up_proj).astype(jnp.bfloat16)
    return lax.dot_general(hidden, hidden, (((0,), (0,)), ((), ())), preferred_element_type=jnp.float32)


def body(tokens, routes, w_gate, w_up):
    owners = lax.axis_size("expert")
    data_ranks = lax.axis_size("dp")
    experts = w_gate.shape[0] * owners
    tok_rows, top_count = routes.shape
    capacity = min(tok_rows, 2 * tok_rows * top_count // experts)
    gate_w, up_w = w_gate[0], w_up[0]
    if tok_rows * owners <= experts * capacity and owners == CHIPS_DENSE * CORES:
        early, late = gathered(tokens, routes, gate_w, up_w)
    else:
        gram = packed_grams(tokens, routes, gate_w, up_w, capacity)
        early, late = gram, []
        for s in range(1, data_ranks):
            early = early + lax.ppermute(gram, "dp", [(r, (r + s) % data_ranks) for r in range(data_ranks)])
    rows_mean = data_ranks * tok_rows * top_count
    return factor_rows(early, late, rows_mean, data_ranks)[None]


def over_lanes(column, width):
    return jnp.concatenate([column] * (width // column.shape[1]), axis=1)


def row_of(x, k):
    return jnp.broadcast_to(x[k : k + 1, :], x.shape)


def lane_of(x, at):
    return jnp.take_along_axis(x, jnp.full(x.shape, at, jnp.int32), axis=1, mode="promise_in_bounds")


PRODUCTS = ((0, 0), (0, 1), (1, 0), (0, 2), (2, 0), (1, 1))


def three_parts(x):
    high = x.astype(jnp.bfloat16).astype(jnp.float32)
    rest = x - high
    middle = rest.astype(jnp.bfloat16).astype(jnp.float32)
    return high, middle, rest - middle


def outer_of_few(a, b):
    left, right = three_parts(a), three_parts(b)
    left = jnp.concatenate([left[i] for i, _ in PRODUCTS], axis=0)
    right = jnp.concatenate([right[j] for _, j in PRODUCTS], axis=0).astype(jnp.bfloat16)
    return jnp.dot(left.T.astype(jnp.bfloat16), right, preferred_element_type=jnp.float32)


def outer_of_many(a, b):
    left, right = three_parts(a.T), three_parts(b)
    left = jnp.concatenate([left[i].astype(jnp.bfloat16) for i, _ in PRODUCTS], axis=1)
    right = jnp.concatenate([right[j].astype(jnp.bfloat16) for _, j in PRODUCTS], axis=0)
    return jnp.dot(left, right, preferred_element_type=jnp.float32)


def factor_panel(rows, column, sublane):
    group, width = rows[0].shape
    count = len(rows)
    extract = lambda u: {t: [column(rows[t], u, j) for j in range(group)] for t in range(u, count)}
    current, done = extract(0), []
    for s in range(count):
        ahead = extract(s + 1) if s + 1 < count else {}
        factor = jnp.zeros_like(rows[s])
        for k in range(group):
            pivot = current[s][k]
            scale = lax.rsqrt(row_of(pivot, k))
            lower = {t: current[t][k] * scale for t in range(s, count)}
            if k + 1 < group:
                current[s][k + 1] = current[s][k + 1] - pivot * row_of(pivot, k + 1) * (scale * scale)
            upper = row_of(rows[s], k) * over_lanes(scale, width)
            factor = jnp.where(sublane == k, upper, factor)
            for j in range(k + 1, group):
                entry = row_of(lower[s], j)
                for t in range(s, count):
                    if (t, j) != (s, k + 1):
                        current[t][j] = current[t][j] - lower[t] * entry
            for j in range(group if ahead else 0):
                entry = row_of(lower[s + 1], j)
                for t in range(s + 1, count):
                    ahead[t][j] = ahead[t][j] - lower[t] * entry
            for t in range(s if k + 1 < group else s + 1, count):
                rows[t] = rows[t] - over_lanes(lower[t], width) * upper
        done.append(factor)
        current = ahead
    return done


def factor_kernel(rank_ref, early_ref, *refs, rows_mean):
    late_refs, (my_rows_ref, out_ref, rest_ref) = refs[:-3], refs[-3:]
    size = early_ref.shape[0]
    block, group, groups = 128, 8, 4
    panel = group * groups
    row = lax.broadcasted_iota(jnp.int32, (size, size), 0)
    col = lax.broadcasted_iota(jnp.int32, (size, size), 1)
    gram = early_ref[...]
    if late_refs:
        gram = gram + gram_of(late_refs)
    rest_ref[...] = gram / rows_mean + jnp.where(row == col, RIDGE, 0.0)
    for base in range(0, size, block):
        width = size - base
        end = base + block
        if base:
            out_ref[base:end, :base] = jnp.zeros((block, base), jnp.float32)
        sublane = lax.broadcasted_iota(jnp.int32, (group, width), 0)
        lane = lax.broadcasted_iota(jnp.int32, (group, width), 1)
        panel_lane = lax.broadcasted_iota(jnp.int32, (panel, block), 1)

        def step(p, carry):
            first = panel * p
            at = [pl.ds(pl.multiple_of(base + first + group * t, group), group) for t in range(groups)]
            rows = [rest_ref[at[t], base:] for t in range(groups)]
            column = lambda x, u, j: lane_of(x[:, :block], first + group * u + j)
            done = factor_panel(rows, column, sublane)
            for t in range(groups):
                out_ref[at[t], base:] = jnp.where(lane >= sublane + first + group * t, done[t], 0.0)
            done = jnp.concatenate(done, axis=0)

            @pl.when(p + 1 < block // panel)
            def _():
                below = jnp.where(panel_lane >= first + panel, done[:, :block], 0.0)
                rest_ref[base:end, base:] -= outer_of_few(below, done)

            return carry

        lax.fori_loop(0, block // panel, step, 0)
        for to in range(end, size, block):
            right = out_ref[base:end, to:]
            rest_ref[to : to + block, to:] -= outer_of_many(right[:, :block], right)
    count = my_rows_ref.shape[0]
    my_rows_ref[...] = out_ref[pl.ds(pl.multiple_of(rank_ref[0] * count, count), count), :]


def factor_rows(early, late, rows_mean, data_ranks):
    size = early.shape[0]
    rank = lax.axis_index("dp").astype(jnp.int32).reshape(1)
    return pl.pallas_call(
        functools.partial(factor_kernel, rows_mean=rows_mean),
        in_specs=[pl.BlockSpec(memory_space=pltpu.SMEM)] + [pl.BlockSpec(memory_space=pltpu.VMEM)] * (1 + len(late)),
        out_specs=pl.BlockSpec(memory_space=pltpu.VMEM),
        out_shape=jax.ShapeDtypeStruct((size // data_ranks, size), jnp.float32),
        scratch_shapes=[pltpu.VMEM((size, size), jnp.float32)] * 2,
        compiler_params=pltpu.CompilerParams(vmem_limit_bytes=24 << 20),
        name="factor",
    )(rank, early, *late)


def solution(mesh):
    in_specs = (
        P(("groups", "dp", "expert"), None),
        P(("groups", "dp", "expert"), None),
        P(("groups", "expert"), None, None),
        P(("groups", "expert"), None, None),
    )
    out_specs = P(("groups", "expert"), "dp", None)
    return jax.shard_map(body, mesh=mesh, in_specs=in_specs, out_specs=out_specs, check_vma=False)
```

```python
import functools

import jax
import jax.numpy as jnp
from jax import lax
from jax.experimental import pallas as pl
from jax.experimental.pallas import tpu as pltpu
from jax.sharding import PartitionSpec as P


RIDGE = 0.05
CORES = 2
CHIPS_DENSE = 4


def hidden_kernel(me_ref, gate_ref, up_ref, *refs, at, top):
    hidden_ref = refs[-1]
    count = len(refs) // 2
    pieces, names = refs[:count], refs[count:-1]
    hw = gate_ref.shape[1]
    width = 256
    member = []
    for name in names:
        hit = (name[at * top : (at + 1) * top, :] == me_ref[0]).astype(jnp.float32)
        member.append(jnp.max(hit.T, axis=1, keepdims=True))
    member = jnp.concatenate(member, axis=0)
    x = jnp.concatenate([piece[...] for piece in pieces], axis=0)

    def step(i, carry):
        columns = pl.ds(pl.multiple_of(i * width, width), width)
        gate = jnp.dot(x, gate_ref[:, columns], preferred_element_type=jnp.float32)
        up = jnp.dot(x, up_ref[:, columns], preferred_element_type=jnp.float32)
        value = gate / (1.0 + jnp.exp(-gate)) * up
        hidden_ref[:, columns] = jnp.where(member > 0, value, 0.0).astype(jnp.bfloat16)
        return carry

    lax.fori_loop(0, hw // width, step, 0)


def hidden_of(me, pieces, names, at, top, gate_w, up_w):
    rows = sum(piece.shape[0] for piece in pieces)
    model, hw = gate_w.shape
    return pl.pallas_call(
        functools.partial(hidden_kernel, at=at, top=top),
        in_specs=[pl.BlockSpec(memory_space=pltpu.SMEM)]
        + [pl.BlockSpec(memory_space=pltpu.VMEM)] * (2 + 2 * len(pieces)),
        out_specs=pl.BlockSpec(memory_space=pltpu.VMEM),
        out_shape=jax.ShapeDtypeStruct((rows, hw), jnp.bfloat16),
        compiler_params=pltpu.CompilerParams(vmem_limit_bytes=24 << 20),
        cost_estimate=pl.CostEstimate(
            flops=2 * rows * model * 2 * hw,
            bytes_accessed=2 * (rows * model + 2 * model * hw) + 2 * rows * hw,
            transcendentals=rows * hw,
        ),
        name="hidden",
    )(me, gate_w, up_w, *pieces, *names)


def gram_of(refs):
    total = None
    for ref in refs:
        h = ref[...]
        part = lax.dot_general(h, h, (((0,), (0,)), ((), ())), preferred_element_type=jnp.float32)
        total = part if total is None else total + part
    return total


def gram_kernel(*refs):
    refs[-1][...] = gram_of(refs[:-1])


def partial_gram(hiddens):
    rows = sum(hidden.shape[0] for hidden in hiddens)
    hw = hiddens[0].shape[1]
    return pl.pallas_call(
        gram_kernel,
        in_specs=[pl.BlockSpec(memory_space=pltpu.VMEM)] * len(hiddens),
        out_specs=pl.BlockSpec(memory_space=pltpu.VMEM),
        out_shape=jax.ShapeDtypeStruct((hw, hw), jnp.float32),
        compiler_params=pltpu.CompilerParams(vmem_limit_bytes=24 << 20),
        cost_estimate=pl.CostEstimate(
            flops=2 * rows * hw * hw,
            bytes_accessed=2 * rows * hw + 4 * hw * hw,
            transcendentals=0,
        ),
        name="partial_gram",
    )(*hiddens)


def between_chips(pairs):
    return [(s * CORES + c, d * CORES + c) for s, d in pairs for c in range(CORES)]


def gathered(tokens, routes, gate_w, up_w):
    me = lax.axis_index("expert").astype(jnp.int32).reshape(1)
    data_ranks = lax.axis_size("dp")
    top = routes.shape[1]
    move = lambda x, pairs: lax.ppermute(x, "expert", between_chips(pairs))
    swap = lambda x: lax.ppermute(x, "expert", [(e, e ^ 1) for e in range(CHIPS_DENSE * CORES)])
    turn = lambda x, s: lax.ppermute(x, "dp", [(r, (r + s) % data_ranks) for r in range(data_ranks)])
    ring = lambda s: [(z, (z + s) % CHIPS_DENSE) for z in range(CHIPS_DENSE)]

    names = routes.T
    above = move(tokens, ring(-1))
    half = tokens.shape[0] // 2
    below, on_up = [], []
    for i in range(2):
        below.append(move(tokens[i * half : (i + 1) * half], ring(1)))
    on_down = move(above, [(2, 1), (1, 0)])
    for i in range(2):
        on_up.append(move(below[i], [(1, 2), (2, 3)]))
    below = jnp.concatenate(below, axis=0)
    moved = []
    for pairs in [ring(-1), ring(1), ring(2)]:
        moved.append(move(names, pairs))
    moved = jnp.concatenate(moved, axis=0)
    other_names = swap(names)
    other_moved = swap(moved)

    hiddens = []
    for slot, own in enumerate([tokens, above, below]):
        other = swap(own)
        who, at = ((names, other_names), 0) if slot == 0 else ((moved, other_moved), slot - 1)
        hidden = hidden_of(me, (own, other), who, at, top, gate_w, up_w)
        hiddens.append([hidden] + [turn(hidden, s) for s in range(1, data_ranks)])
    early = partial_gram(sum(hiddens, []))

    last = jnp.concatenate(on_up, axis=0) + on_down
    other = swap(last)
    late = []
    for piece, who in ((last, moved), (other, other_moved)):
        hidden = hidden_of(me, (piece,), (who,), 2, top, gate_w, up_w)
        late += [hidden] + [turn(hidden, s) for s in range(1, data_ranks)]
    return early, late


def packed_grams(tokens, routes, gate_w, up_w, capacity):
    owners = lax.axis_size("expert")
    experts = owners
    model_width = tokens.shape[1]
    tok_rows, top_count = routes.shape
    assigned = routes.reshape(-1)
    onehot = (assigned[:, None] == jnp.arange(experts, dtype=jnp.int32)[None, :]).astype(jnp.int32)
    position = jnp.sum(jnp.cumsum(onehot, axis=0) * onehot, axis=1) - 1
    target = assigned * capacity + position
    anchor = jnp.arange(tok_rows * top_count, dtype=jnp.int32) // top_count
    source_row = jnp.zeros((experts * capacity,), jnp.int32).at[target].set(anchor)
    filled = jnp.zeros((experts * capacity,), jnp.int32).at[target].set(1)
    outbox = jnp.where(filled[:, None] > 0, tokens[source_row], jnp.zeros((), tokens.dtype))
    outbox = outbox.reshape(experts, capacity, model_width)
    arrived = lax.all_to_all(outbox, "expert", split_axis=0, concat_axis=0, tiled=True)
    flattened = arrived.reshape(-1, model_width)
    gate_proj = jnp.dot(flattened, gate_w, preferred_element_type=jnp.float32)
    up_proj = jnp.dot(flattened, up_w, preferred_element_type=jnp.float32)
    hidden = (jax.nn.silu(gate_proj) * up_proj).astype(jnp.bfloat16)
    return lax.dot_general(hidden, hidden, (((0,), (0,)), ((), ())), preferred_element_type=jnp.float32)


def body(tokens, routes, w_gate, w_up):
    owners = lax.axis_size("expert")
    data_ranks = lax.axis_size("dp")
    experts = w_gate.shape[0] * owners
    tok_rows, top_count = routes.shape
    capacity = min(tok_rows, 2 * tok_rows * top_count // experts)
    gate_w, up_w = w_gate[0], w_up[0]
    if tok_rows * owners <= experts * capacity and owners == CHIPS_DENSE * CORES:
        early, late = gathered(tokens, routes, gate_w, up_w)
    else:
        gram = packed_grams(tokens, routes, gate_w, up_w, capacity)
        early, late = gram, []
        for s in range(1, data_ranks):
            early = early + lax.ppermute(gram, "dp", [(r, (r + s) % data_ranks) for r in range(data_ranks)])
    rows_mean = data_ranks * tok_rows * top_count
    return factor_rows(early, late, rows_mean, data_ranks)[None]


def over_lanes(column, width):
    return jnp.concatenate([column] * (width // column.shape[1]), axis=1)


def row_of(x, k):
    return jnp.broadcast_to(x[k : k + 1, :], x.shape)


def lane_of(x, at):
    return jnp.take_along_axis(x, jnp.full(x.shape, at, jnp.int32), axis=1, mode="promise_in_bounds")


PRODUCTS = ((0, 0), (0, 1), (1, 0), (0, 2), (2, 0), (1, 1))


def three_parts(x):
    high = x.astype(jnp.bfloat16).astype(jnp.float32)
    rest = x - high
    middle = rest.astype(jnp.bfloat16).astype(jnp.float32)
    return high, middle, rest - middle


def outer_of_few(a, b):
    left, right = three_parts(a), three_parts(b)
    left = jnp.concatenate([left[i] for i, _ in PRODUCTS], axis=0)
    right = jnp.concatenate([right[j] for _, j in PRODUCTS], axis=0).astype(jnp.bfloat16)
    return jnp.dot(left.T.astype(jnp.bfloat16), right, preferred_element_type=jnp.float32)


def outer_of_many(a, b):
    left, right = three_parts(a.T), three_parts(b)
    left = jnp.concatenate([left[i].astype(jnp.bfloat16) for i, _ in PRODUCTS], axis=1)
    right = jnp.concatenate([right[j].astype(jnp.bfloat16) for _, j in PRODUCTS], axis=0)
    return jnp.dot(left, right, preferred_element_type=jnp.float32)


def factor_panel(rows, column, sublane):
    group, width = rows[0].shape
    count = len(rows)
    extract = lambda u: {t: [column(rows[t], u, j) for j in range(group)] for t in range(u, count)}
    current, done = extract(0), []
    for s in range(count):
        ahead = extract(s + 1) if s + 1 < count else {}
        factor = jnp.zeros_like(rows[s])
        for k in range(group):
            pivot = current[s][k]
            scale = lax.rsqrt(row_of(pivot, k))
            lower = {t: current[t][k] * scale for t in range(s, count)}
            if k + 1 < group:
                current[s][k + 1] = current[s][k + 1] - pivot * row_of(pivot, k + 1) * (scale * scale)
            upper = row_of(rows[s], k) * over_lanes(scale, width)
            factor = jnp.where(sublane == k, upper, factor)
            for j in range(k + 1, group):
                entry = row_of(lower[s], j)
                for t in range(s, count):
                    if (t, j) != (s, k + 1):
                        current[t][j] = current[t][j] - lower[t] * entry
            for j in range(group if ahead else 0):
                entry = row_of(lower[s + 1], j)
                for t in range(s + 1, count):
                    ahead[t][j] = ahead[t][j] - lower[t] * entry
            for t in range(s if k + 1 < group else s + 1, count):
                rows[t] = rows[t] - over_lanes(lower[t], width) * upper
        done.append(factor)
        current = ahead
    return done


def factor_kernel(rank_ref, early_ref, *refs, rows_mean):
    late_refs, (my_rows_ref, out_ref, rest_ref) = refs[:-3], refs[-3:]
    size = early_ref.shape[0]
    block, group, groups = 128, 8, 4
    panel = group * groups
    row = lax.broadcasted_iota(jnp.int32, (size, size), 0)
    col = lax.broadcasted_iota(jnp.int32, (size, size), 1)
    gram = early_ref[...]
    if late_refs:
        gram = gram + gram_of(late_refs)
    rest_ref[...] = gram / rows_mean + jnp.where(row == col, RIDGE, 0.0)
    for base in range(0, size, block):
        width = size - base
        end = base + block
        if base:
            out_ref[base:end, :base] = jnp.zeros((block, base), jnp.float32)
        sublane = lax.broadcasted_iota(jnp.int32, (group, width), 0)
        lane = lax.broadcasted_iota(jnp.int32, (group, width), 1)
        panel_lane = lax.broadcasted_iota(jnp.int32, (panel, block), 1)

        def step(p, carry):
            first = panel * p
            at = [pl.ds(pl.multiple_of(base + first + group * t, group), group) for t in range(groups)]
            rows = [rest_ref[at[t], base:] for t in range(groups)]
            column = lambda x, u, j: lane_of(x[:, :block], first + group * u + j)
            done = factor_panel(rows, column, sublane)
            for t in range(groups):
                out_ref[at[t], base:] = jnp.where(lane >= sublane + first + group * t, done[t], 0.0)
            done = jnp.concatenate(done, axis=0)

            @pl.when(p + 1 < block // panel)
            def _():
                below = jnp.where(panel_lane >= first + panel, done[:, :block], 0.0)
                rest_ref[base:end, base:] -= outer_of_few(below, done)

            return carry

        lax.fori_loop(0, block // panel, step, 0)
        for to in range(end, size, block):
            right = out_ref[base:end, to:]
            rest_ref[to : to + block, to:] -= outer_of_many(right[:, :block], right)
    count = my_rows_ref.shape[0]
    my_rows_ref[...] = out_ref[pl.ds(pl.multiple_of(rank_ref[0] * count, count), count), :]


def factor_rows(early, late, rows_mean, data_ranks):
    size = early.shape[0]
    rank = lax.axis_index("dp").astype(jnp.int32).reshape(1)
    return pl.pallas_call(
        functools.partial(factor_kernel, rows_mean=rows_mean),
        in_specs=[pl.BlockSpec(memory_space=pltpu.SMEM)] + [pl.BlockSpec(memory_space=pltpu.VMEM)] * (1 + len(late)),
        out_specs=pl.BlockSpec(memory_space=pltpu.VMEM),
        out_shape=jax.ShapeDtypeStruct((size // data_ranks, size), jnp.float32),
        scratch_shapes=[pltpu.VMEM((size, size), jnp.float32)] * 2,
        compiler_params=pltpu.CompilerParams(vmem_limit_bytes=24 << 20),
        name="factor",
    )(rank, early, *late)


def solution(mesh):
    in_specs = (
        P(("groups", "dp", "expert"), None),
        P(("groups", "dp", "expert"), None),
        P(("groups", "expert"), None, None),
        P(("groups", "expert"), None, None),
    )
    out_specs = P(("groups", "expert"), "dp", None)
    return jax.shard_map(body, mesh=mesh, in_specs=in_specs, out_specs=out_specs, check_vma=False)
```

```python
import functools

import jax
import jax.numpy as jnp
from jax import lax
from jax.experimental import pallas as pl
from jax.experimental.pallas import tpu as pltpu
from jax.sharding import PartitionSpec as P


RIDGE = 0.05
CORES = 2
CHIPS_DENSE = 4


def hidden_kernel(me_ref, gate_ref, up_ref, *refs, at, top):
    hidden_ref = refs[-1]
    count = len(refs) // 2
    pieces, names = refs[:count], refs[count:-1]
    hw = gate_ref.shape[1]
    width = 256
    member = []
    for name in names:
        hit = (name[at * top : (at + 1) * top, :] == me_ref[0]).astype(jnp.float32)
        member.append(jnp.max(hit.T, axis=1, keepdims=True))
    member = jnp.concatenate(member, axis=0)
    x = jnp.concatenate([piece[...] for piece in pieces], axis=0)

    def step(i, carry):
        columns = pl.ds(pl.multiple_of(i * width, width), width)
        gate = jnp.dot(x, gate_ref[:, columns], preferred_element_type=jnp.float32)
        up = jnp.dot(x, up_ref[:, columns], preferred_element_type=jnp.float32)
        value = gate / (1.0 + jnp.exp(-gate)) * up
        hidden_ref[:, columns] = jnp.where(member > 0, value, 0.0).astype(jnp.bfloat16)
        return carry

    lax.fori_loop(0, hw // width, step, 0)


def hidden_of(me, pieces, names, at, top, gate_w, up_w):
    rows = sum(piece.shape[0] for piece in pieces)
    model, hw = gate_w.shape
    return pl.pallas_call(
        functools.partial(hidden_kernel, at=at, top=top),
        in_specs=[pl.BlockSpec(memory_space=pltpu.SMEM)]
        + [pl.BlockSpec(memory_space=pltpu.VMEM)] * (2 + 2 * len(pieces)),
        out_specs=pl.BlockSpec(memory_space=pltpu.VMEM),
        out_shape=jax.ShapeDtypeStruct((rows, hw), jnp.bfloat16),
        compiler_params=pltpu.CompilerParams(vmem_limit_bytes=24 << 20),
        cost_estimate=pl.CostEstimate(
            flops=2 * rows * model * 2 * hw,
            bytes_accessed=2 * (rows * model + 2 * model * hw) + 2 * rows * hw,
            transcendentals=rows * hw,
        ),
        name="hidden",
    )(me, gate_w, up_w, *pieces, *names)


def gram_of(refs):
    h = jnp.concatenate([ref[...] for ref in refs], axis=0)
    return lax.dot_general(h, h, (((0,), (0,)), ((), ())), preferred_element_type=jnp.float32)


def gram_kernel(*refs):
    refs[-1][...] = gram_of(refs[:-1])


def partial_gram(hiddens):
    rows = sum(hidden.shape[0] for hidden in hiddens)
    hw = hiddens[0].shape[1]
    return pl.pallas_call(
        gram_kernel,
        in_specs=[pl.BlockSpec(memory_space=pltpu.VMEM)] * len(hiddens),
        out_specs=pl.BlockSpec(memory_space=pltpu.VMEM),
        out_shape=jax.ShapeDtypeStruct((hw, hw), jnp.float32),
        compiler_params=pltpu.CompilerParams(vmem_limit_bytes=24 << 20),
        cost_estimate=pl.CostEstimate(
            flops=2 * rows * hw * hw,
            bytes_accessed=2 * rows * hw + 4 * hw * hw,
            transcendentals=0,
        ),
        name="partial_gram",
    )(*hiddens)


def between_chips(pairs):
    return [(s * CORES + c, d * CORES + c) for s, d in pairs for c in range(CORES)]


def gathered(tokens, routes, gate_w, up_w):
    me = lax.axis_index("expert").astype(jnp.int32).reshape(1)
    data_ranks = lax.axis_size("dp")
    top = routes.shape[1]
    move = lambda x, pairs: lax.ppermute(x, "expert", between_chips(pairs))
    swap = lambda x: lax.ppermute(x, "expert", [(e, e ^ 1) for e in range(CHIPS_DENSE * CORES)])
    turn = lambda x, s: lax.ppermute(x, "dp", [(r, (r + s) % data_ranks) for r in range(data_ranks)])
    ring = lambda s: [(z, (z + s) % CHIPS_DENSE) for z in range(CHIPS_DENSE)]

    names = routes.T
    above = move(tokens, ring(-1))
    half = tokens.shape[0] // 2
    below, on_up = [], []
    for i in range(2):
        below.append(move(tokens[i * half : (i + 1) * half], ring(1)))
    on_down = move(above, [(2, 1), (1, 0)])
    for i in range(2):
        on_up.append(move(below[i], [(1, 2), (2, 3)]))
    below = jnp.concatenate(below, axis=0)
    moved = []
    for pairs in [ring(-1), ring(1), ring(2)]:
        moved.append(move(names, pairs))
    moved = jnp.concatenate(moved, axis=0)
    other_names = swap(names)
    other_moved = swap(moved)

    hiddens = []
    for slot, own in enumerate([tokens, above, below]):
        other = swap(own)
        who, at = ((names, other_names), 0) if slot == 0 else ((moved, other_moved), slot - 1)
        hidden = hidden_of(me, (own, other), who, at, top, gate_w, up_w)
        hiddens.append([hidden] + [turn(hidden, s) for s in range(1, data_ranks)])
    early = partial_gram(sum(hiddens, []))

    last = jnp.concatenate(on_up, axis=0) + on_down
    other = swap(last)
    late = []
    for piece, who in ((last, moved), (other, other_moved)):
        hidden = hidden_of(me, (piece,), (who,), 2, top, gate_w, up_w)
        late += [hidden] + [turn(hidden, s) for s in range(1, data_ranks)]
    return early, late


def packed_grams(tokens, routes, gate_w, up_w, capacity):
    owners = lax.axis_size("expert")
    experts = owners
    model_width = tokens.shape[1]
    tok_rows, top_count = routes.shape
    assigned = routes.reshape(-1)
    onehot = (assigned[:, None] == jnp.arange(experts, dtype=jnp.int32)[None, :]).astype(jnp.int32)
    position = jnp.sum(jnp.cumsum(onehot, axis=0) * onehot, axis=1) - 1
    target = assigned * capacity + position
    anchor = jnp.arange(tok_rows * top_count, dtype=jnp.int32) // top_count
    source_row = jnp.zeros((experts * capacity,), jnp.int32).at[target].set(anchor)
    filled = jnp.zeros((experts * capacity,), jnp.int32).at[target].set(1)
    outbox = jnp.where(filled[:, None] > 0, tokens[source_row], jnp.zeros((), tokens.dtype))
    outbox = outbox.reshape(experts, capacity, model_width)
    arrived = lax.all_to_all(outbox, "expert", split_axis=0, concat_axis=0, tiled=True)
    flattened = arrived.reshape(-1, model_width)
    gate_proj = jnp.dot(flattened, gate_w, preferred_element_type=jnp.float32)
    up_proj = jnp.dot(flattened, up_w, preferred_element_type=jnp.float32)
    hidden = (jax.nn.silu(gate_proj) * up_proj).astype(jnp.bfloat16)
    return lax.dot_general(hidden, hidden, (((0,), (0,)), ((), ())), preferred_element_type=jnp.float32)


def body(tokens, routes, w_gate, w_up):
    owners = lax.axis_size("expert")
    data_ranks = lax.axis_size("dp")
    experts = w_gate.shape[0] * owners
    tok_rows, top_count = routes.shape
    capacity = min(tok_rows, 2 * tok_rows * top_count // experts)
    gate_w, up_w = w_gate[0], w_up[0]
    if tok_rows * owners <= experts * capacity and owners == CHIPS_DENSE * CORES:
        early, late = gathered(tokens, routes, gate_w, up_w)
    else:
        gram = packed_grams(tokens, routes, gate_w, up_w, capacity)
        early, late = gram, []
        for s in range(1, data_ranks):
            early = early + lax.ppermute(gram, "dp", [(r, (r + s) % data_ranks) for r in range(data_ranks)])
    rows_mean = data_ranks * tok_rows * top_count
    return factor_rows(early, late, rows_mean, data_ranks)[None]


def over_lanes(column, width):
    return jnp.concatenate([column] * (width // column.shape[1]), axis=1)


def row_of(x, k):
    return jnp.broadcast_to(x[k : k + 1, :], x.shape)


PRODUCTS = ((0, 0), (0, 1), (1, 0), (0, 2), (2, 0), (1, 1))


def three_parts(x):
    high = x.astype(jnp.bfloat16).astype(jnp.float32)
    rest = x - high
    middle = rest.astype(jnp.bfloat16).astype(jnp.float32)
    return high, middle, rest - middle


def outer_of_few(a, b):
    left, right = three_parts(a), three_parts(b)
    left = jnp.concatenate([left[i] for i, _ in PRODUCTS], axis=0)
    right = jnp.concatenate([right[j] for _, j in PRODUCTS], axis=0).astype(jnp.bfloat16)
    return jnp.dot(left.T.astype(jnp.bfloat16), right, preferred_element_type=jnp.float32)


def outer_of_many(a, b):
    left, right = three_parts(a.T), three_parts(b)
    left = jnp.concatenate([left[i].astype(jnp.bfloat16) for i, _ in PRODUCTS], axis=1)
    right = jnp.concatenate([right[j].astype(jnp.bfloat16) for _, j in PRODUCTS], axis=0)
    return jnp.dot(left, right, preferred_element_type=jnp.float32)


def factor_panel(rows, column, sublane):
    group, width = rows[0].shape
    count = len(rows)
    extract = lambda u: {t: [column(rows[t], u, j) for j in range(group)] for t in range(u, count)}
    current, done = extract(0), []
    for s in range(count):
        ahead = extract(s + 1) if s + 1 < count else {}
        factor = jnp.zeros_like(rows[s])
        for k in range(group):
            pivot = current[s][k]
            scale = lax.rsqrt(row_of(pivot, k))
            lower = {t: current[t][k] * scale for t in range(s, count)}
            if k + 1 < group:
                current[s][k + 1] = current[s][k + 1] - pivot * row_of(pivot, k + 1) * (scale * scale)
            upper = row_of(rows[s], k) * over_lanes(scale, width)
            factor = jnp.where(sublane == k, upper, factor)
            for j in range(k + 1, group):
                entry = row_of(lower[s], j)
                for t in range(s, count):
                    if (t, j) != (s, k + 1):
                        current[t][j] = current[t][j] - lower[t] * entry
            for j in range(group if ahead else 0):
                entry = row_of(lower[s + 1], j)
                for t in range(s + 1, count):
                    ahead[t][j] = ahead[t][j] - lower[t] * entry
            for t in range(s if k + 1 < group else s + 1, count):
                rows[t] = rows[t] - over_lanes(lower[t], width) * upper
        done.append(factor)
        current = ahead
    return done


def factor_kernel(rank_ref, early_ref, *refs, rows_mean):
    late_refs, (my_rows_ref, out_ref, rest_ref) = refs[:-3], refs[-3:]
    size = early_ref.shape[0]
    block, group, groups = 128, 8, 4
    panel = group * groups
    row = lax.broadcasted_iota(jnp.int32, (size, size), 0)
    col = lax.broadcasted_iota(jnp.int32, (size, size), 1)
    gram = early_ref[...]
    if late_refs:
        gram = gram + gram_of(late_refs)
    rest_ref[...] = gram / rows_mean + jnp.where(row == col, RIDGE, 0.0)
    for base in range(0, size, block):
        width = size - base
        end = base + block
        if base:
            out_ref[base:end, :base] = jnp.zeros((block, base), jnp.float32)
        sublane = lax.broadcasted_iota(jnp.int32, (group, width), 0)
        lane = lax.broadcasted_iota(jnp.int32, (group, width), 1)
        column = lambda x, at: jnp.broadcast_to(x[:, at : at + 1], (group, block))
        for first in range(0, block, panel):
            at = [slice(base + first + group * t, base + first + group * (t + 1)) for t in range(groups)]
            rows = [rest_ref[at[t], base:] for t in range(groups)]
            done = factor_panel(rows, lambda x, u, j: column(x, first + group * u + j), sublane)
            for t in range(groups):
                out_ref[at[t], base:] = jnp.where(lane >= sublane + first + group * t, done[t], 0.0)
            after = first + panel
            if after < block:
                done = jnp.concatenate(done, axis=0)
                rest_ref[base + after : end, base:] -= outer_of_few(done[:, :block], done)[after:, :]
        for to in range(end, size, block):
            right = out_ref[base:end, to:]
            rest_ref[to : to + block, to:] -= outer_of_many(right[:, :block], right)
    count = my_rows_ref.shape[0]
    my_rows_ref[...] = out_ref[pl.ds(pl.multiple_of(rank_ref[0] * count, count), count), :]


def factor_rows(early, late, rows_mean, data_ranks):
    size = early.shape[0]
    rank = lax.axis_index("dp").astype(jnp.int32).reshape(1)
    return pl.pallas_call(
        functools.partial(factor_kernel, rows_mean=rows_mean),
        in_specs=[pl.BlockSpec(memory_space=pltpu.SMEM)] + [pl.BlockSpec(memory_space=pltpu.VMEM)] * (1 + len(late)),
        out_specs=pl.BlockSpec(memory_space=pltpu.VMEM),
        out_shape=jax.ShapeDtypeStruct((size // data_ranks, size), jnp.float32),
        scratch_shapes=[pltpu.VMEM((size, size), jnp.float32)] * 2,
        compiler_params=pltpu.CompilerParams(vmem_limit_bytes=24 << 20),
        name="factor",
    )(rank, early, *late)


def solution(mesh):
    in_specs = (
        P(("groups", "dp", "expert"), None),
        P(("groups", "dp", "expert"), None),
        P(("groups", "expert"), None, None),
        P(("groups", "expert"), None, None),
    )
    out_specs = P(("groups", "expert"), "dp", None)
    return jax.shard_map(body, mesh=mesh, in_specs=in_specs, out_specs=out_specs, check_vma=False)
```

```python
import functools

import jax
import jax.numpy as jnp
from jax import lax
from jax.experimental import pallas as pl
from jax.experimental.pallas import tpu as pltpu
from jax.sharding import PartitionSpec as P


RIDGE = 0.05
CORES = 2
CHIPS_DENSE = 4


def hidden_kernel(me_ref, gate_ref, up_ref, *refs, at, top, first):
    hidden_ref = refs[-1]
    count = len(refs) // 2
    pieces, names = refs[:count], refs[count:-1]
    hw = gate_ref.shape[1]
    width = 256
    member = []
    for piece, name in zip(pieces, names):
        hit = (name[at * top : (at + 1) * top, :] == me_ref[0]).astype(jnp.float32)
        member.append(jnp.max(hit.T[first : first + piece.shape[0], :], axis=1, keepdims=True))
    member = jnp.concatenate(member, axis=0)
    x = jnp.concatenate([piece[...] for piece in pieces], axis=0)

    def step(i, carry):
        columns = pl.ds(pl.multiple_of(i * width, width), width)
        gate = jnp.dot(x, gate_ref[:, columns], preferred_element_type=jnp.float32)
        up = jnp.dot(x, up_ref[:, columns], preferred_element_type=jnp.float32)
        value = gate / (1.0 + jnp.exp(-gate)) * up
        hidden_ref[:, columns] = jnp.where(member > 0, value, 0.0).astype(jnp.bfloat16)
        return carry

    lax.fori_loop(0, hw // width, step, 0)


def hidden_of(me, pieces, names, at, top, first, gate_w, up_w):
    rows = sum(piece.shape[0] for piece in pieces)
    model, hw = gate_w.shape
    return pl.pallas_call(
        functools.partial(hidden_kernel, at=at, top=top, first=first),
        in_specs=[pl.BlockSpec(memory_space=pltpu.SMEM)]
        + [pl.BlockSpec(memory_space=pltpu.VMEM)] * (2 + 2 * len(pieces)),
        out_specs=pl.BlockSpec(memory_space=pltpu.VMEM),
        out_shape=jax.ShapeDtypeStruct((rows, hw), jnp.bfloat16),
        compiler_params=pltpu.CompilerParams(vmem_limit_bytes=6 << 20),
        cost_estimate=pl.CostEstimate(
            flops=2 * rows * model * 2 * hw,
            bytes_accessed=2 * (rows * model + 2 * model * hw) + 2 * rows * hw,
            transcendentals=rows * hw,
        ),
        name="hidden",
    )(me, gate_w, up_w, *pieces, *names)


def gram_of(refs):
    h = jnp.concatenate([ref[...] for ref in refs], axis=0)
    return lax.dot_general(h, h, (((0,), (0,)), ((), ())), preferred_element_type=jnp.float32)


def gram_kernel(*refs):
    refs[-1][...] = gram_of(refs[:-1])


def partial_gram(hiddens):
    rows = sum(hidden.shape[0] for hidden in hiddens)
    hw = hiddens[0].shape[1]
    return pl.pallas_call(
        gram_kernel,
        in_specs=[pl.BlockSpec(memory_space=pltpu.VMEM)] * len(hiddens),
        out_specs=pl.BlockSpec(memory_space=pltpu.VMEM),
        out_shape=jax.ShapeDtypeStruct((hw, hw), jnp.float32),
        compiler_params=pltpu.CompilerParams(vmem_limit_bytes=6 << 20),
        cost_estimate=pl.CostEstimate(
            flops=2 * rows * hw * hw,
            bytes_accessed=2 * rows * hw + 4 * hw * hw,
            transcendentals=0,
        ),
        name="partial_gram",
    )(*hiddens)


def between_chips(pairs):
    return [(s * CORES + c, d * CORES + c) for s, d in pairs for c in range(CORES)]


def gathered(tokens, routes, gate_w, up_w):
    me = lax.axis_index("expert").astype(jnp.int32).reshape(1)
    data_ranks = lax.axis_size("dp")
    top = routes.shape[1]
    move = lambda x, pairs: lax.ppermute(x, "expert", between_chips(pairs))
    swap = lambda x: lax.ppermute(x, "expert", [(e, e ^ 1) for e in range(CHIPS_DENSE * CORES)])
    turn = lambda x, s: lax.ppermute(x, "dp", [(r, (r + s) % data_ranks) for r in range(data_ranks)])
    ring = lambda s: [(z, (z + s) % CHIPS_DENSE) for z in range(CHIPS_DENSE)]

    names = routes.T
    above = move(tokens, ring(-1))
    half = tokens.shape[0] // 2
    below, on_up, on_down = [], [], []
    for i in range(2):
        below.append(move(tokens[i * half : (i + 1) * half], ring(1)))
    for i in range(2):
        on_down.append(move(above[i * half : (i + 1) * half], [(2, 1), (1, 0)]))
    for i in range(2):
        on_up.append(move(below[i], [(1, 2), (2, 3)]))
    below = jnp.concatenate(below, axis=0)
    moved = []
    for pairs in [ring(-1), ring(1), ring(2)]:
        moved.append(move(names, pairs))
    moved = jnp.concatenate(moved, axis=0)
    other_names = swap(names)
    other_moved = swap(moved)

    hiddens = []
    for slot, own in enumerate([tokens, above, below]):
        other = swap(own)
        who, at = ((names, other_names), 0) if slot == 0 else ((moved, other_moved), slot - 1)
        hidden = hidden_of(me, (own, other), who, at, top, 0, gate_w, up_w)
        hiddens.append([hidden] + [turn(hidden, s) for s in range(1, data_ranks)])
    early = partial_gram(sum(hiddens, []))

    late = []
    slot = 3
    for i in range(2):
        last = on_up[i] + on_down[i]
        other = swap(last)
        pieces = [((last, other), (moved, other_moved))] if i == 0 else [((last,), (moved,)), ((other,), (other_moved,))]
        for piece, who in pieces:
            hidden = hidden_of(me, piece, who, 2, top, i * half, gate_w, up_w)
            late += [hidden] + [turn(hidden, s) for s in range(1, data_ranks)]
            slot += 1
    return early, late


def packed_grams(tokens, routes, gate_w, up_w, capacity):
    owners = lax.axis_size("expert")
    experts = owners
    model_width = tokens.shape[1]
    tok_rows, top_count = routes.shape
    assigned = routes.reshape(-1)
    onehot = (assigned[:, None] == jnp.arange(experts, dtype=jnp.int32)[None, :]).astype(jnp.int32)
    position = jnp.sum(jnp.cumsum(onehot, axis=0) * onehot, axis=1) - 1
    target = assigned * capacity + position
    anchor = jnp.arange(tok_rows * top_count, dtype=jnp.int32) // top_count
    source_row = jnp.zeros((experts * capacity,), jnp.int32).at[target].set(anchor)
    filled = jnp.zeros((experts * capacity,), jnp.int32).at[target].set(1)
    outbox = jnp.where(filled[:, None] > 0, tokens[source_row], jnp.zeros((), tokens.dtype))
    outbox = outbox.reshape(experts, capacity, model_width)
    arrived = lax.all_to_all(outbox, "expert", split_axis=0, concat_axis=0, tiled=True)
    flattened = arrived.reshape(-1, model_width)
    gate_proj = jnp.dot(flattened, gate_w, preferred_element_type=jnp.float32)
    up_proj = jnp.dot(flattened, up_w, preferred_element_type=jnp.float32)
    hidden = (jax.nn.silu(gate_proj) * up_proj).astype(jnp.bfloat16)
    return lax.dot_general(hidden, hidden, (((0,), (0,)), ((), ())), preferred_element_type=jnp.float32)


def body(tokens, routes, w_gate, w_up):
    owners = lax.axis_size("expert")
    data_ranks = lax.axis_size("dp")
    experts = w_gate.shape[0] * owners
    tok_rows, top_count = routes.shape
    capacity = min(tok_rows, 2 * tok_rows * top_count // experts)
    gate_w, up_w = w_gate[0], w_up[0]
    if tok_rows * owners <= experts * capacity and owners == CHIPS_DENSE * CORES:
        early, late = gathered(tokens, routes, gate_w, up_w)
    else:
        gram = packed_grams(tokens, routes, gate_w, up_w, capacity)
        early, late = gram, []
        for s in range(1, data_ranks):
            early = early + lax.ppermute(gram, "dp", [(r, (r + s) % data_ranks) for r in range(data_ranks)])
    rows_mean = data_ranks * tok_rows * top_count
    return factor_rows(early, late, rows_mean, data_ranks)[None]


def over_lanes(column, width):
    return jnp.concatenate([column] * (width // column.shape[1]), axis=1)


def row_of(x, k):
    return jnp.broadcast_to(x[k : k + 1, :], x.shape)


PRODUCTS = ((0, 0), (0, 1), (1, 0), (0, 2), (2, 0), (1, 1))


def three_parts(x):
    high = x.astype(jnp.bfloat16).astype(jnp.float32)
    rest = x - high
    middle = rest.astype(jnp.bfloat16).astype(jnp.float32)
    return high, middle, rest - middle


def outer_of_few(a, b):
    left, right = three_parts(a), three_parts(b)
    left = jnp.concatenate([left[i] for i, _ in PRODUCTS], axis=0)
    right = jnp.concatenate([right[j] for _, j in PRODUCTS], axis=0).astype(jnp.bfloat16)
    return jnp.dot(left.T.astype(jnp.bfloat16), right, preferred_element_type=jnp.float32)


def outer_of_many(a, b):
    left, right = three_parts(a.T), three_parts(b)
    left = jnp.concatenate([left[i].astype(jnp.bfloat16) for i, _ in PRODUCTS], axis=1)
    right = jnp.concatenate([right[j].astype(jnp.bfloat16) for _, j in PRODUCTS], axis=0)
    return jnp.dot(left, right, preferred_element_type=jnp.float32)


def factor_panel(rows, column, sublane):
    group, width = rows[0].shape
    count = len(rows)
    extract = lambda u: {t: [column(rows[t], u, j) for j in range(group)] for t in range(u, count)}
    current, done = extract(0), []
    for s in range(count):
        ahead = extract(s + 1) if s + 1 < count else {}
        factor = jnp.zeros_like(rows[s])
        for k in range(group):
            pivot = current[s][k]
            scale = lax.rsqrt(row_of(pivot, k))
            lower = {t: current[t][k] * scale for t in range(s, count)}
            if k + 1 < group:
                current[s][k + 1] = current[s][k + 1] - pivot * row_of(pivot, k + 1) * (scale * scale)
            upper = row_of(rows[s], k) * over_lanes(scale, width)
            factor = jnp.where(sublane == k, upper, factor)
            for j in range(k + 1, group):
                entry = row_of(lower[s], j)
                for t in range(s, count):
                    if (t, j) != (s, k + 1):
                        current[t][j] = current[t][j] - lower[t] * entry
            for j in range(group if ahead else 0):
                entry = row_of(lower[s + 1], j)
                for t in range(s + 1, count):
                    ahead[t][j] = ahead[t][j] - lower[t] * entry
            for t in range(s if k + 1 < group else s + 1, count):
                rows[t] = rows[t] - over_lanes(lower[t], width) * upper
        done.append(factor)
        current = ahead
    return done


def factor_kernel(rank_ref, early_ref, *refs, rows_mean):
    late_refs, (my_rows_ref, out_ref, rest_ref) = refs[:-3], refs[-3:]
    size = early_ref.shape[0]
    block, group, groups = 128, 8, 4
    panel = group * groups
    row = lax.broadcasted_iota(jnp.int32, (size, size), 0)
    col = lax.broadcasted_iota(jnp.int32, (size, size), 1)
    gram = early_ref[...]
    if late_refs:
        gram = gram + gram_of(late_refs)
    rest_ref[...] = gram / rows_mean + jnp.where(row == col, RIDGE, 0.0)
    for base in range(0, size, block):
        width = size - base
        end = base + block
        if base:
            out_ref[base:end, :base] = jnp.zeros((block, base), jnp.float32)
        sublane = lax.broadcasted_iota(jnp.int32, (group, width), 0)
        lane = lax.broadcasted_iota(jnp.int32, (group, width), 1)
        column = lambda x, at: jnp.broadcast_to(x[:, at : at + 1], (group, block))
        for first in range(0, block, panel):
            at = [slice(base + first + group * t, base + first + group * (t + 1)) for t in range(groups)]
            rows = [rest_ref[at[t], base:] for t in range(groups)]
            done = factor_panel(rows, lambda x, u, j: column(x, first + group * u + j), sublane)
            for t in range(groups):
                out_ref[at[t], base:] = jnp.where(lane >= sublane + first + group * t, done[t], 0.0)
            after = first + panel
            if after < block:
                done = jnp.concatenate(done, axis=0)
                rest_ref[base + after : end, base:] -= outer_of_few(done[:, :block], done)[after:, :]
        for to in range(end, size, block):
            right = out_ref[base:end, to:]
            rest_ref[to : to + block, to:] -= outer_of_many(right[:, :block], right)
    count = my_rows_ref.shape[0]
    my_rows_ref[...] = out_ref[pl.ds(pl.multiple_of(rank_ref[0] * count, count), count), :]


def factor_rows(early, late, rows_mean, data_ranks):
    size = early.shape[0]
    rank = lax.axis_index("dp").astype(jnp.int32).reshape(1)
    return pl.pallas_call(
        functools.partial(factor_kernel, rows_mean=rows_mean),
        in_specs=[pl.BlockSpec(memory_space=pltpu.SMEM)] + [pl.BlockSpec(memory_space=pltpu.VMEM)] * (1 + len(late)),
        out_specs=pl.BlockSpec(memory_space=pltpu.VMEM),
        out_shape=jax.ShapeDtypeStruct((size // data_ranks, size), jnp.float32),
        scratch_shapes=[pltpu.VMEM((size, size), jnp.float32)] * 2,
        compiler_params=pltpu.CompilerParams(vmem_limit_bytes=6 << 20),
        name="factor",
    )(rank, early, *late)


def solution(mesh):
    in_specs = (
        P(("groups", "dp", "expert"), None),
        P(("groups", "dp", "expert"), None),
        P(("groups", "expert"), None, None),
        P(("groups", "expert"), None, None),
    )
    out_specs = P(("groups", "expert"), "dp", None)
    return jax.shard_map(body, mesh=mesh, in_specs=in_specs, out_specs=out_specs, check_vma=False)
```

```python
import functools

import jax
import jax.numpy as jnp
from jax import lax
from jax.experimental import pallas as pl
from jax.experimental.pallas import tpu as pltpu
from jax.sharding import PartitionSpec as P


RIDGE = 0.05
CORES = 2
CHIPS_DENSE = 4


def hidden_kernel(me_ref, gate_ref, up_ref, *refs, at, top):
    hidden_ref = refs[-1]
    count = len(refs) // 2
    pieces, names = refs[:count], refs[count:-1]
    hw = gate_ref.shape[1]
    width = 256
    member = []
    for name in names:
        hit = (name[at * top : (at + 1) * top, :] == me_ref[0]).astype(jnp.float32)
        member.append(jnp.max(hit.T, axis=1, keepdims=True))
    member = jnp.concatenate(member, axis=0)
    x = jnp.concatenate([piece[...] for piece in pieces], axis=0)

    for i in range(hw // width):
        columns = slice(i * width, (i + 1) * width)
        gate = jnp.dot(x, gate_ref[:, columns], preferred_element_type=jnp.float32)
        up = jnp.dot(x, up_ref[:, columns], preferred_element_type=jnp.float32)
        value = gate / (1.0 + jnp.exp(-gate)) * up
        hidden_ref[:, columns] = jnp.where(member > 0, value, 0.0).astype(jnp.bfloat16)


def hidden_of(me, pieces, names, at, top, gate_w, up_w):
    rows = sum(piece.shape[0] for piece in pieces)
    model, hw = gate_w.shape
    return pl.pallas_call(
        functools.partial(hidden_kernel, at=at, top=top),
        in_specs=[pl.BlockSpec(memory_space=pltpu.SMEM)]
        + [pl.BlockSpec(memory_space=pltpu.VMEM)] * (2 + 2 * len(pieces)),
        out_specs=pl.BlockSpec(memory_space=pltpu.VMEM),
        out_shape=jax.ShapeDtypeStruct((rows, hw), jnp.bfloat16),
        compiler_params=pltpu.CompilerParams(vmem_limit_bytes=24 << 20),
        cost_estimate=pl.CostEstimate(
            flops=2 * rows * model * 2 * hw,
            bytes_accessed=2 * (rows * model + 2 * model * hw) + 2 * rows * hw,
            transcendentals=rows * hw,
        ),
        name="hidden",
    )(me, gate_w, up_w, *pieces, *names)


def gram_of(refs):
    h = jnp.concatenate([ref[...] for ref in refs], axis=0)
    return lax.dot_general(h, h, (((0,), (0,)), ((), ())), preferred_element_type=jnp.float32)


def gram_kernel(*refs):
    refs[-1][...] = gram_of(refs[:-1])


def partial_gram(hiddens):
    rows = sum(hidden.shape[0] for hidden in hiddens)
    hw = hiddens[0].shape[1]
    return pl.pallas_call(
        gram_kernel,
        in_specs=[pl.BlockSpec(memory_space=pltpu.VMEM)] * len(hiddens),
        out_specs=pl.BlockSpec(memory_space=pltpu.VMEM),
        out_shape=jax.ShapeDtypeStruct((hw, hw), jnp.float32),
        compiler_params=pltpu.CompilerParams(vmem_limit_bytes=24 << 20),
        cost_estimate=pl.CostEstimate(
            flops=2 * rows * hw * hw,
            bytes_accessed=2 * rows * hw + 4 * hw * hw,
            transcendentals=0,
        ),
        name="partial_gram",
    )(*hiddens)


def between_chips(pairs):
    return [(s * CORES + c, d * CORES + c) for s, d in pairs for c in range(CORES)]


def gathered(tokens, routes, gate_w, up_w):
    me = lax.axis_index("expert").astype(jnp.int32).reshape(1)
    data_ranks = lax.axis_size("dp")
    top = routes.shape[1]
    move = lambda x, pairs: lax.ppermute(x, "expert", between_chips(pairs))
    swap = lambda x: lax.ppermute(x, "expert", [(e, e ^ 1) for e in range(CHIPS_DENSE * CORES)])
    turn = lambda x, s: lax.ppermute(x, "dp", [(r, (r + s) % data_ranks) for r in range(data_ranks)])
    ring = lambda s: [(z, (z + s) % CHIPS_DENSE) for z in range(CHIPS_DENSE)]

    names = routes.T
    above = move(tokens, ring(-1))
    half = tokens.shape[0] // 2
    below, on_up = [], []
    for i in range(2):
        below.append(move(tokens[i * half : (i + 1) * half], ring(1)))
    on_down = move(above, [(2, 1), (1, 0)])
    for i in range(2):
        on_up.append(move(below[i], [(1, 2), (2, 3)]))
    below = jnp.concatenate(below, axis=0)
    moved = []
    for pairs in [ring(-1), ring(1), ring(2)]:
        moved.append(move(names, pairs))
    moved = jnp.concatenate(moved, axis=0)
    other_names = swap(names)
    other_moved = swap(moved)

    hiddens = []
    for slot, own in enumerate([tokens, above, below]):
        other = swap(own)
        who, at = ((names, other_names), 0) if slot == 0 else ((moved, other_moved), slot - 1)
        hidden = hidden_of(me, (own, other), who, at, top, gate_w, up_w)
        hiddens.append([hidden] + [turn(hidden, s) for s in range(1, data_ranks)])
    early = partial_gram(sum(hiddens, []))

    last = jnp.concatenate(on_up, axis=0) + on_down
    other = swap(last)
    late = []
    for piece, who in ((last, moved), (other, other_moved)):
        hidden = hidden_of(me, (piece,), (who,), 2, top, gate_w, up_w)
        late += [hidden] + [turn(hidden, s) for s in range(1, data_ranks)]
    return early, late


def packed_grams(tokens, routes, gate_w, up_w, capacity):
    owners = lax.axis_size("expert")
    experts = owners
    model_width = tokens.shape[1]
    tok_rows, top_count = routes.shape
    assigned = routes.reshape(-1)
    onehot = (assigned[:, None] == jnp.arange(experts, dtype=jnp.int32)[None, :]).astype(jnp.int32)
    position = jnp.sum(jnp.cumsum(onehot, axis=0) * onehot, axis=1) - 1
    target = assigned * capacity + position
    anchor = jnp.arange(tok_rows * top_count, dtype=jnp.int32) // top_count
    source_row = jnp.zeros((experts * capacity,), jnp.int32).at[target].set(anchor)
    filled = jnp.zeros((experts * capacity,), jnp.int32).at[target].set(1)
    outbox = jnp.where(filled[:, None] > 0, tokens[source_row], jnp.zeros((), tokens.dtype))
    outbox = outbox.reshape(experts, capacity, model_width)
    arrived = lax.all_to_all(outbox, "expert", split_axis=0, concat_axis=0, tiled=True)
    flattened = arrived.reshape(-1, model_width)
    gate_proj = jnp.dot(flattened, gate_w, preferred_element_type=jnp.float32)
    up_proj = jnp.dot(flattened, up_w, preferred_element_type=jnp.float32)
    hidden = (jax.nn.silu(gate_proj) * up_proj).astype(jnp.bfloat16)
    return lax.dot_general(hidden, hidden, (((0,), (0,)), ((), ())), preferred_element_type=jnp.float32)


def body(tokens, routes, w_gate, w_up):
    owners = lax.axis_size("expert")
    data_ranks = lax.axis_size("dp")
    experts = w_gate.shape[0] * owners
    tok_rows, top_count = routes.shape
    capacity = min(tok_rows, 2 * tok_rows * top_count // experts)
    gate_w, up_w = w_gate[0], w_up[0]
    if tok_rows * owners <= experts * capacity and owners == CHIPS_DENSE * CORES:
        early, late = gathered(tokens, routes, gate_w, up_w)
    else:
        gram = packed_grams(tokens, routes, gate_w, up_w, capacity)
        early, late = gram, []
        for s in range(1, data_ranks):
            early = early + lax.ppermute(gram, "dp", [(r, (r + s) % data_ranks) for r in range(data_ranks)])
    rows_mean = data_ranks * tok_rows * top_count
    return factor_rows(early, late, rows_mean, data_ranks)[None]


def over_lanes(column, width):
    return jnp.concatenate([column] * (width // column.shape[1]), axis=1)


def row_of(x, k):
    return jnp.broadcast_to(x[k : k + 1, :], x.shape)


PRODUCTS = ((0, 0), (0, 1), (1, 0), (0, 2), (2, 0), (1, 1))


def three_parts(x):
    high = x.astype(jnp.bfloat16).astype(jnp.float32)
    rest = x - high
    middle = rest.astype(jnp.bfloat16).astype(jnp.float32)
    return high, middle, rest - middle


def outer_of_few(a, b):
    left, right = three_parts(a), three_parts(b)
    left = jnp.concatenate([left[i] for i, _ in PRODUCTS], axis=0)
    right = jnp.concatenate([right[j] for _, j in PRODUCTS], axis=0).astype(jnp.bfloat16)
    return jnp.dot(left.T.astype(jnp.bfloat16), right, preferred_element_type=jnp.float32)


def stacked_parts(a, side, axis):
    parts = [part.astype(jnp.bfloat16) for part in three_parts(a)]
    return jnp.concatenate([parts[product[side]] for product in PRODUCTS], axis=axis)


def factor_panel(rows, column, sublane):
    group, width = rows[0].shape
    count = len(rows)
    extract = lambda u: {t: [column(rows[t], u, j) for j in range(group)] for t in range(u, count)}
    current, done = extract(0), []
    for s in range(count):
        ahead = extract(s + 1) if s + 1 < count else {}
        factor = jnp.zeros_like(rows[s])
        for k in range(group):
            pivot = current[s][k]
            scale = lax.rsqrt(row_of(pivot, k))
            lower = {t: current[t][k] * scale for t in range(s, count)}
            if k + 1 < group:
                current[s][k + 1] = current[s][k + 1] - pivot * row_of(pivot, k + 1) * (scale * scale)
            upper = row_of(rows[s], k) * over_lanes(scale, width)
            factor = jnp.where(sublane == k, upper, factor)
            for j in range(k + 1, group):
                entry = row_of(lower[s], j)
                for t in range(s, count):
                    if (t, j) != (s, k + 1):
                        current[t][j] = current[t][j] - lower[t] * entry
            for j in range(group if ahead else 0):
                entry = row_of(lower[s + 1], j)
                for t in range(s + 1, count):
                    ahead[t][j] = ahead[t][j] - lower[t] * entry
            for t in range(s if k + 1 < group else s + 1, count):
                rows[t] = rows[t] - over_lanes(lower[t], width) * upper
        done.append(factor)
        current = ahead
    return done


def factor_kernel(rank_ref, early_ref, *refs, rows_mean):
    late_refs, (my_rows_ref, out_ref, rest_ref) = refs[:-3], refs[-3:]
    size = early_ref.shape[0]
    block, group, groups = 128, 8, 4
    panel = group * groups
    row = lax.broadcasted_iota(jnp.int32, (size, size), 0)
    col = lax.broadcasted_iota(jnp.int32, (size, size), 1)
    gram = early_ref[...]
    if late_refs:
        gram = gram + gram_of(late_refs)
    rest_ref[...] = gram / rows_mean + jnp.where(row == col, RIDGE, 0.0)
    for base in range(0, size, block):
        width = size - base
        end = base + block
        if base:
            out_ref[base:end, :base] = jnp.zeros((block, base), jnp.float32)
        sublane = lax.broadcasted_iota(jnp.int32, (group, width), 0)
        lane = lax.broadcasted_iota(jnp.int32, (group, width), 1)
        column = lambda x, at: jnp.broadcast_to(x[:, at : at + 1], (group, block))
        for first in range(0, block, panel):
            at = [slice(base + first + group * t, base + first + group * (t + 1)) for t in range(groups)]
            rows = [rest_ref[at[t], base:] for t in range(groups)]
            done = factor_panel(rows, lambda x, u, j: column(x, first + group * u + j), sublane)
            for t in range(groups):
                out_ref[at[t], base:] = jnp.where(lane >= sublane + first + group * t, done[t], 0.0)
            after = first + panel
            if after < block:
                done = jnp.concatenate(done, axis=0)
                rest_ref[base + after : end, base:] -= outer_of_few(done[:, :block], done)[after:, :]
        if end < size:
            right = stacked_parts(out_ref[base:end, end:], 1, 0)
        for to in range(end, size, block):
            left = stacked_parts(out_ref[base:end, to : to + block].T, 0, 1)
            rest_ref[to : to + block, to:] -= jnp.dot(
                left, right[:, to - end :], preferred_element_type=jnp.float32
            )
    count = my_rows_ref.shape[0]
    my_rows_ref[...] = out_ref[pl.ds(pl.multiple_of(rank_ref[0] * count, count), count), :]


def factor_rows(early, late, rows_mean, data_ranks):
    size = early.shape[0]
    rank = lax.axis_index("dp").astype(jnp.int32).reshape(1)
    return pl.pallas_call(
        functools.partial(factor_kernel, rows_mean=rows_mean),
        in_specs=[pl.BlockSpec(memory_space=pltpu.SMEM)] + [pl.BlockSpec(memory_space=pltpu.VMEM)] * (1 + len(late)),
        out_specs=pl.BlockSpec(memory_space=pltpu.VMEM),
        out_shape=jax.ShapeDtypeStruct((size // data_ranks, size), jnp.float32),
        scratch_shapes=[pltpu.VMEM((size, size), jnp.float32)] * 2,
        compiler_params=pltpu.CompilerParams(vmem_limit_bytes=24 << 20),
        name="factor",
    )(rank, early, *late)


def solution(mesh):
    in_specs = (
        P(("groups", "dp", "expert"), None),
        P(("groups", "dp", "expert"), None),
        P(("groups", "expert"), None, None),
        P(("groups", "expert"), None, None),
    )
    out_specs = P(("groups", "expert"), "dp", None)
    return jax.shard_map(body, mesh=mesh, in_specs=in_specs, out_specs=out_specs, check_vma=False)
```

```python
import functools

import jax
import jax.numpy as jnp
from jax import lax
from jax.experimental import pallas as pl
from jax.experimental.pallas import tpu as pltpu
from jax.sharding import PartitionSpec as P


RIDGE = 0.05
CORES = 2
CHIPS_DENSE = 4


def hidden_kernel(me_ref, gate_ref, up_ref, *refs, at, top):
    hidden_ref = refs[-1]
    count = len(refs) // 2
    pieces, names = refs[:count], refs[count:-1]
    hw = gate_ref.shape[1]
    width = 256
    member = []
    for name in names:
        hit = (name[at * top : (at + 1) * top, :] == me_ref[0]).astype(jnp.float32)
        member.append(jnp.max(hit.T, axis=1, keepdims=True))
    member = jnp.concatenate(member, axis=0)
    x = jnp.concatenate([piece[...] for piece in pieces], axis=0)

    for i in range(hw // width):
        columns = slice(i * width, (i + 1) * width)
        gate = jnp.dot(x, gate_ref[:, columns], preferred_element_type=jnp.float32)
        up = jnp.dot(x, up_ref[:, columns], preferred_element_type=jnp.float32)
        value = gate / (1.0 + jnp.exp(-gate)) * up
        hidden_ref[:, columns] = jnp.where(member > 0, value, 0.0).astype(jnp.bfloat16)


def hidden_of(me, pieces, names, at, top, gate_w, up_w):
    rows = sum(piece.shape[0] for piece in pieces)
    model, hw = gate_w.shape
    return pl.pallas_call(
        functools.partial(hidden_kernel, at=at, top=top),
        in_specs=[pl.BlockSpec(memory_space=pltpu.SMEM)]
        + [pl.BlockSpec(memory_space=pltpu.VMEM)] * (2 + 2 * len(pieces)),
        out_specs=pl.BlockSpec(memory_space=pltpu.VMEM),
        out_shape=jax.ShapeDtypeStruct((rows, hw), jnp.bfloat16),
        compiler_params=pltpu.CompilerParams(vmem_limit_bytes=24 << 20),
        cost_estimate=pl.CostEstimate(
            flops=2 * rows * model * 2 * hw,
            bytes_accessed=2 * (rows * model + 2 * model * hw) + 2 * rows * hw,
            transcendentals=rows * hw,
        ),
        name="hidden",
    )(me, gate_w, up_w, *pieces, *names)


def gram_of(refs):
    h = jnp.concatenate([ref[...] for ref in refs], axis=0)
    return lax.dot_general(h, h, (((0,), (0,)), ((), ())), preferred_element_type=jnp.float32)


def gram_kernel(*refs, count):
    gram = gram_of(refs[:count])
    refs[-1][...] = gram if len(refs) == count + 1 else refs[count][...] + gram


def partial_gram(hiddens, *total):
    rows = sum(hidden.shape[0] for hidden in hiddens)
    hw = hiddens[0].shape[1]
    return pl.pallas_call(
        functools.partial(gram_kernel, count=len(hiddens)),
        in_specs=[pl.BlockSpec(memory_space=pltpu.VMEM)] * (len(hiddens) + len(total)),
        out_specs=pl.BlockSpec(memory_space=pltpu.VMEM),
        out_shape=jax.ShapeDtypeStruct((hw, hw), jnp.float32),
        compiler_params=pltpu.CompilerParams(vmem_limit_bytes=24 << 20),
        cost_estimate=pl.CostEstimate(
            flops=2 * rows * hw * hw,
            bytes_accessed=2 * rows * hw + 4 * hw * hw,
            transcendentals=0,
        ),
        name="partial_gram",
    )(*hiddens, *total)


def between_chips(pairs):
    return [(s * CORES + c, d * CORES + c) for s, d in pairs for c in range(CORES)]


def gathered(tokens, routes, gate_w, up_w):
    me = lax.axis_index("expert").astype(jnp.int32).reshape(1)
    data_ranks = lax.axis_size("dp")
    top = routes.shape[1]
    move = lambda x, pairs: lax.ppermute(x, "expert", between_chips(pairs))
    swap = lambda x: lax.ppermute(x, "expert", [(e, e ^ 1) for e in range(CHIPS_DENSE * CORES)])
    turn = lambda x, s: lax.ppermute(x, "dp", [(r, (r + s) % data_ranks) for r in range(data_ranks)])
    ring = lambda s: [(z, (z + s) % CHIPS_DENSE) for z in range(CHIPS_DENSE)]

    names = routes.T
    above = move(tokens, ring(-1))
    half = tokens.shape[0] // 2
    below, on_up = [], []
    for i in range(2):
        below.append(move(tokens[i * half : (i + 1) * half], ring(1)))
    on_down = move(above, [(2, 1), (1, 0)])
    for i in range(2):
        on_up.append(move(below[i], [(1, 2), (2, 3)]))
    below = jnp.concatenate(below, axis=0)
    moved = []
    for pairs in [ring(-1), ring(1), ring(2)]:
        moved.append(move(names, pairs))
    moved = jnp.concatenate(moved, axis=0)
    other_names = swap(names)
    other_moved = swap(moved)

    hiddens = []
    for slot, own in enumerate([tokens, above, below]):
        other = swap(own)
        who, at = ((names, other_names), 0) if slot == 0 else ((moved, other_moved), slot - 1)
        hidden = hidden_of(me, (own, other), who, at, top, gate_w, up_w)
        hiddens.append([hidden] + [turn(hidden, s) for s in range(1, data_ranks)])
    early = partial_gram(sum(hiddens, []))

    last = jnp.concatenate(on_up, axis=0) + on_down
    other = swap(last)
    late = []
    for piece, who in ((last, moved), (other, other_moved)):
        hidden = hidden_of(me, (piece,), (who,), 2, top, gate_w, up_w)
        late.append([hidden] + [turn(hidden, s) for s in range(1, data_ranks)])
    early = partial_gram(late[0] + late[1][:1], early)
    return early, late[1][1:]


def packed_grams(tokens, routes, gate_w, up_w, capacity):
    owners = lax.axis_size("expert")
    experts = owners
    model_width = tokens.shape[1]
    tok_rows, top_count = routes.shape
    assigned = routes.reshape(-1)
    onehot = (assigned[:, None] == jnp.arange(experts, dtype=jnp.int32)[None, :]).astype(jnp.int32)
    position = jnp.sum(jnp.cumsum(onehot, axis=0) * onehot, axis=1) - 1
    target = assigned * capacity + position
    anchor = jnp.arange(tok_rows * top_count, dtype=jnp.int32) // top_count
    source_row = jnp.zeros((experts * capacity,), jnp.int32).at[target].set(anchor)
    filled = jnp.zeros((experts * capacity,), jnp.int32).at[target].set(1)
    outbox = jnp.where(filled[:, None] > 0, tokens[source_row], jnp.zeros((), tokens.dtype))
    outbox = outbox.reshape(experts, capacity, model_width)
    arrived = lax.all_to_all(outbox, "expert", split_axis=0, concat_axis=0, tiled=True)
    flattened = arrived.reshape(-1, model_width)
    gate_proj = jnp.dot(flattened, gate_w, preferred_element_type=jnp.float32)
    up_proj = jnp.dot(flattened, up_w, preferred_element_type=jnp.float32)
    hidden = (jax.nn.silu(gate_proj) * up_proj).astype(jnp.bfloat16)
    return lax.dot_general(hidden, hidden, (((0,), (0,)), ((), ())), preferred_element_type=jnp.float32)


def body(tokens, routes, w_gate, w_up):
    owners = lax.axis_size("expert")
    data_ranks = lax.axis_size("dp")
    experts = w_gate.shape[0] * owners
    tok_rows, top_count = routes.shape
    capacity = min(tok_rows, 2 * tok_rows * top_count // experts)
    gate_w, up_w = w_gate[0], w_up[0]
    if tok_rows * owners <= experts * capacity and owners == CHIPS_DENSE * CORES:
        early, late = gathered(tokens, routes, gate_w, up_w)
    else:
        gram = packed_grams(tokens, routes, gate_w, up_w, capacity)
        early, late = gram, []
        for s in range(1, data_ranks):
            early = early + lax.ppermute(gram, "dp", [(r, (r + s) % data_ranks) for r in range(data_ranks)])
    rows_mean = data_ranks * tok_rows * top_count
    return factor_rows(early, late, rows_mean, data_ranks)[None]


def over_lanes(column, width):
    return jnp.concatenate([column] * (width // column.shape[1]), axis=1)


def row_of(x, k):
    return jnp.broadcast_to(x[k : k + 1, :], x.shape)


PRODUCTS = ((0, 0), (0, 1), (1, 0), (0, 2), (2, 0), (1, 1))


def three_parts(x):
    high = x.astype(jnp.bfloat16).astype(jnp.float32)
    rest = x - high
    middle = rest.astype(jnp.bfloat16).astype(jnp.float32)
    return high, middle, rest - middle


def outer_of_few(a, b):
    left, right = three_parts(a), three_parts(b)
    left = jnp.concatenate([left[i] for i, _ in PRODUCTS], axis=0)
    right = jnp.concatenate([right[j] for _, j in PRODUCTS], axis=0).astype(jnp.bfloat16)
    return jnp.dot(left.T.astype(jnp.bfloat16), right, preferred_element_type=jnp.float32)


def stacked_parts(a, side, axis):
    parts = [part.astype(jnp.bfloat16) for part in three_parts(a)]
    return jnp.concatenate([parts[product[side]] for product in PRODUCTS], axis=axis)


def factor_panel(rows, column, sublane):
    group, width = rows[0].shape
    count = len(rows)
    extract = lambda u: {t: [column(rows[t], u, j) for j in range(group)] for t in range(u, count)}
    current, done = extract(0), []
    for s in range(count):
        ahead = extract(s + 1) if s + 1 < count else {}
        factor = jnp.zeros_like(rows[s])
        for k in range(group):
            pivot = current[s][k]
            scale = lax.rsqrt(row_of(pivot, k))
            lower = {t: current[t][k] * scale for t in range(s, count)}
            if k + 1 < group:
                current[s][k + 1] = current[s][k + 1] - pivot * row_of(pivot, k + 1) * (scale * scale)
            upper = row_of(rows[s], k) * over_lanes(scale, width)
            factor = jnp.where(sublane == k, upper, factor)
            for j in range(k + 1, group):
                entry = row_of(lower[s], j)
                for t in range(s, count):
                    if (t, j) != (s, k + 1):
                        current[t][j] = current[t][j] - lower[t] * entry
            for j in range(group if ahead else 0):
                entry = row_of(lower[s + 1], j)
                for t in range(s + 1, count):
                    ahead[t][j] = ahead[t][j] - lower[t] * entry
            for t in range(s if k + 1 < group else s + 1, count):
                rows[t] = rows[t] - over_lanes(lower[t], width) * upper
        done.append(factor)
        current = ahead
    return done


def factor_kernel(rank_ref, early_ref, *refs, rows_mean):
    late_refs, (my_rows_ref, out_ref, rest_ref) = refs[:-3], refs[-3:]
    size = early_ref.shape[0]
    block, group, groups = 128, 8, 4
    panel = group * groups
    late = jnp.concatenate([ref[...] for ref in late_refs], axis=0) if late_refs else None
    for base in range(0, size, block):
        corner = slice(base, base + block)
        gram = early_ref[corner, base:]
        if late is not None:
            gram = gram + lax.dot_general(
                late[:, corner], late[:, base:], (((0,), (0,)), ((), ())), preferred_element_type=jnp.float32
            )
        row = lax.broadcasted_iota(jnp.int32, gram.shape, 0)
        col = lax.broadcasted_iota(jnp.int32, gram.shape, 1)
        rest_ref[corner, base:] = gram / rows_mean + jnp.where(row == col, RIDGE, 0.0)
    for base in range(0, size, block):
        width = size - base
        end = base + block
        if base:
            out_ref[base:end, :base] = jnp.zeros((block, base), jnp.float32)
        sublane = lax.broadcasted_iota(jnp.int32, (group, width), 0)
        lane = lax.broadcasted_iota(jnp.int32, (group, width), 1)
        column = lambda x, at: jnp.broadcast_to(x[:, at : at + 1], (group, block))
        for first in range(0, block, panel):
            at = [slice(base + first + group * t, base + first + group * (t + 1)) for t in range(groups)]
            rows = [rest_ref[at[t], base:] for t in range(groups)]
            done = factor_panel(rows, lambda x, u, j: column(x, first + group * u + j), sublane)
            for t in range(groups):
                out_ref[at[t], base:] = jnp.where(lane >= sublane + first + group * t, done[t], 0.0)
            after = first + panel
            if after < block:
                done = jnp.concatenate(done, axis=0)
                rest_ref[base + after : end, base:] -= outer_of_few(done[:, :block], done)[after:, :]
        if end < size:
            right = stacked_parts(out_ref[base:end, end:], 1, 0)
        for to in range(end, size, block):
            left = stacked_parts(out_ref[base:end, to : to + block].T, 0, 1)
            rest_ref[to : to + block, to:] -= jnp.dot(
                left, right[:, to - end :], preferred_element_type=jnp.float32
            )
    count = my_rows_ref.shape[0]
    my_rows_ref[...] = out_ref[pl.ds(pl.multiple_of(rank_ref[0] * count, count), count), :]


def factor_rows(early, late, rows_mean, data_ranks):
    size = early.shape[0]
    rank = lax.axis_index("dp").astype(jnp.int32).reshape(1)
    return pl.pallas_call(
        functools.partial(factor_kernel, rows_mean=rows_mean),
        in_specs=[pl.BlockSpec(memory_space=pltpu.SMEM)] + [pl.BlockSpec(memory_space=pltpu.VMEM)] * (1 + len(late)),
        out_specs=pl.BlockSpec(memory_space=pltpu.VMEM),
        out_shape=jax.ShapeDtypeStruct((size // data_ranks, size), jnp.float32),
        scratch_shapes=[pltpu.VMEM((size, size), jnp.float32)] * 2,
        compiler_params=pltpu.CompilerParams(vmem_limit_bytes=24 << 20),
        name="factor",
    )(rank, early, *late)


def solution(mesh):
    in_specs = (
        P(("groups", "dp", "expert"), None),
        P(("groups", "dp", "expert"), None),
        P(("groups", "expert"), None, None),
        P(("groups", "expert"), None, None),
    )
    out_specs = P(("groups", "expert"), "dp", None)
    return jax.shard_map(body, mesh=mesh, in_specs=in_specs, out_specs=out_specs, check_vma=False)
```
